512 devices in a mesh: req: 128 (over z, y, core), tp: 4 (over x).
Axes of the slice: x: 4, y: 4, z: 16, core: 2. Of those that a mesh axis runs over, the one named last changes fastest.
Arguments:
- query: bfloat16 [512, 2048], P('req', 'tp'), may hold values from -8 to 8
- key_new: bfloat16 [512, 2048], P('req', 'tp'), may hold values from -4 to 4
- value_new: bfloat16 [512, 2048], P('req', 'tp'), may hold values from -4 to 4
- resid: bfloat16 [512, 2048], P('req', 'tp'), may hold values from -6 to 6
- lengths: int32 [512], replicated, may hold values from 1 to 512, as said below
- owner: int32 [512], replicated, may hold values from 0 to 127, as said below
- page_table: int32 [512, 16], replicated, may hold values from 0 to 21, as said below
- kv_pool: bfloat16 [2, 2816, 32, 2048], P(None, 'req', None, 'tp'), may hold values from -4 to 4
- out_weight: bfloat16 [2048, 2048], P('tp'), may hold values from -0.125 to 0.125
- out_bias: bfloat16 [2048], P('tp'), may hold values from -3 to 3
- norm_gain: bfloat16 [2048], P('tp'), may hold values from 0.099609375 to 1.8984375
- norm_bias: bfloat16 [2048], P('tp'), may hold values from -3 to 3
- up_weight_t: bfloat16 [8192, 2048], P('req', 'tp'), may hold values from -0.125 to 0.125
- up_bias: bfloat16 [8192], P('req'), may hold values from -3 to 3
- down_weight: bfloat16 [8192, 2048], P('req', 'tp'), may hold values from -0.0625 to 0.0625
- down_bias: bfloat16 [2048], P('tp'), may hold values from -3 to 3
- order: int32 [512], replicated, may hold values from 0 to 511, each once
Outputs:
- layer_out: bfloat16 [512, 2048], P('req', 'tp')
The draws below stay inside these ranges and needn't reach their ends.
Inputs may be any that keep to these rules, and one draw needn't show every extreme that they name: `lengths`: one request in 32 (at least one) is long, with a length from 256 to 512; the others have at most 63 positions. `owner`: every index of req owns exactly 4 requests, at most one of them long, and no two of them among the 4 rows that one index of req holds. `page_table`: entry j of request r for j < ceil(lengths[r] / 32) names a page of the owner's pool that no other entry of that owner's requests below that bound names; later entries are arbitrary pages.
All inputs are finite; a program needn't handle non-finite values.
Results may differ from the reference program's by a relative error of at most 0.015.
Values may be sent and summed in bfloat16 or wider, within the bound.
A program may use at most 64 MiB of HBM per device.

```python
import math
import jax
import jax.numpy as jnp
from jax import lax

D = 2048
HEADS = 16
HEAD_DIM = 128
FF = 8192
REQ_DEV = 4
PAGE = 32
LONG = 512
REQS = 512
MAXP = 16
POOL = 22
SHORT = 63
N_REQ = 128


def plan(key):
    base_key = jax.random.fold_in(key, 11)
    key_dev, key_off, key_col, key_short, key_long, key_pool = jax.random.split(base_key, 6)
    long_count = max(REQS // 32, 1)
    dev_perm = jax.random.permutation(key_dev, N_REQ).astype(jnp.int32)
    dev_inverse = jnp.zeros((N_REQ,), jnp.int32).at[dev_perm].set(jnp.arange(N_REQ, dtype=jnp.int32))
    offsets = jax.random.permutation(key_off, N_REQ).astype(jnp.int32)[:REQ_DEV]
    col_perm = jax.vmap(lambda sub: jax.random.permutation(sub, REQ_DEV).astype(jnp.int32))(jax.random.split(key_col, N_REQ))
    slots = jnp.arange(REQS, dtype=jnp.int32)
    slot_dev = slots // REQ_DEV
    slot_rank = slots % REQ_DEV
    source = (dev_inverse[slot_dev] - offsets[slot_rank]) % N_REQ
    slot_req = (source * REQ_DEV + col_perm[source, slot_rank]).astype(jnp.int32)
    owner = jnp.zeros((REQS,), jnp.int32).at[slot_req].set(slot_dev)
    long_ids = slot_req.reshape(N_REQ, REQ_DEV)[dev_perm[:long_count], 0]
    is_long = jnp.zeros((REQS,), jnp.int32).at[long_ids].set(1)
    short_len = jax.random.randint(key_short, (REQS,), 1, SHORT + 1).astype(jnp.int32)
    long_len = jax.random.randint(key_long, (REQS,), LONG // 2, LONG + 1).astype(jnp.int32)
    lengths = jnp.where(is_long == 1, long_len, short_len)
    lengths = lengths.at[long_ids[0]].set(LONG)
    slot_len = lengths[slot_req]
    grid_pages = ((slot_len + PAGE - 1) // PAGE).reshape(N_REQ, REQ_DEV)
    offset = jnp.cumsum(grid_pages, axis=1) - grid_pages
    used_total = jnp.sum(grid_pages, axis=1, keepdims=True)
    unused = MAXP - grid_pages
    unused_offset = jnp.cumsum(unused, axis=1) - unused
    entry = jnp.arange(MAXP, dtype=jnp.int32)[None, None, :]
    used_place = offset[:, :, None] + entry
    spare_place = used_total[:, :, None] + unused_offset[:, :, None] + (entry - grid_pages[:, :, None])
    place = jnp.where(entry < grid_pages[:, :, None], used_place, spare_place) % POOL
    pool_perm = jax.vmap(lambda sub: jax.random.permutation(sub, POOL).astype(jnp.int32))(jax.random.split(key_pool, N_REQ))
    page_ids = jnp.take_along_axis(pool_perm, place.reshape(N_REQ, REQ_DEV * MAXP), axis=1)
    table = jnp.zeros((REQS, MAXP), jnp.int32).at[slot_req].set(page_ids.reshape(REQS, MAXP))
    return (lengths, owner, table)


def draw_lengths(key, part):
    return plan(key)[0]


def draw_owner(key, part):
    return plan(key)[1]


def draw_page_table(key, part):
    return plan(key)[2]


def draw_query(key, part):
    fresh = jax.random.fold_in(key, 31)
    shape = (REQS, HEADS * HEAD_DIM)
    return jnp.clip(jax.random.normal(fresh, shape, jnp.float32), -6.0, 6.0).astype(jnp.bfloat16)


def draw_kv_pool(key, part):
    fresh = jax.random.fold_in(key, 41)
    shape = (2, N_REQ * POOL, PAGE, HEADS * HEAD_DIM)
    return jnp.clip(jax.random.normal(fresh, shape, jnp.float32), -4.0, 4.0).astype(jnp.bfloat16)


def block_levels(stream_key, extent, cuts, smallest, high):
    def one(position, shards_of):
        steps = jax.random.uniform(jax.random.fold_in(jax.random.fold_in(stream_key, 6), position), (shards_of,), jnp.float32, smallest / len(cuts), high / len(cuts))
        return jnp.repeat(jnp.exp(steps), extent[position] // shards_of).reshape((-1,) + (1,) * (len(extent) - position - 1))

    level = one(*cuts[0])
    for cut in cuts[1:]:
        level = level * one(*cut)
    return level


def bell_draw(own_key, dims, width, bound, cuts=(), kind=jnp.bfloat16):
    values = jax.random.normal(own_key, dims, jnp.float32) * width
    if len(cuts) > 0:
        values = block_levels(own_key, dims, cuts, -0.22, 0.18) * values
    return jnp.clip(values, min=-bound, max=bound).astype(kind)


def setup_inputs(seed: int = 0) -> dict:
    splits = jax.random.split(jax.random.key(seed), 18)
    return {
        "query": draw_query(jax.random.fold_in(splits[17], 71), 0),
        "key_new": bell_draw(splits[1], (REQS, HEADS * HEAD_DIM), 1.0, 4.0, ((0, 128), (1, 4))),
        "value_new": bell_draw(splits[2], (REQS, HEADS * HEAD_DIM), 1.0, 4.0, ((0, 128), (1, 4))),
        "resid": bell_draw(splits[3], (REQS, D), 1.0, 6.0, ((0, 128), (1, 4))),
        "lengths": draw_lengths(jax.random.fold_in(splits[17], 71), 0),
        "owner": draw_owner(jax.random.fold_in(splits[17], 71), 0),
        "page_table": draw_page_table(jax.random.fold_in(splits[17], 71), 0),
        "kv_pool": draw_kv_pool(jax.random.fold_in(splits[17], 71), 0),
        "out_weight": bell_draw(splits[8], (HEADS * HEAD_DIM, D), D ** -0.5, 0.125, ((0, 4),)),
        "out_bias": bell_draw(splits[9], (D,), 0.5, 3.0, ((0, 4),)),
        "norm_gain": jnp.clip(1.0 + 0.18 * jax.random.normal(splits[10], (D,), jnp.float32), 0.099609375, 1.8984375).astype(jnp.bfloat16),
        "norm_bias": bell_draw(splits[11], (D,), 0.5, 3.0, ((0, 4),)),
        "up_weight_t": bell_draw(splits[12], (FF, D), D ** -0.5, 0.125, ((0, 128), (1, 4))),
        "up_bias": bell_draw(splits[13], (FF,), 0.5, 3.0, ((0, 128),)),
        "down_weight": bell_draw(splits[14], (FF, D), FF ** -0.5, 0.0625, ((0, 128), (1, 4))),
        "down_bias": bell_draw(splits[15], (D,), 0.5, 3.0, ((0, 4),)),
        "order": jax.random.permutation(splits[16], REQS).astype(jnp.int32),
    }


def reference(query, key_new, value_new, resid, lengths, owner, page_table, kv_pool, out_weight, out_bias, norm_gain, norm_bias, up_weight_t, up_bias, down_weight, down_bias, order):
    score_scale = 1.0 / math.sqrt(HEAD_DIM)
    span = MAXP * PAGE
    highest = lax.Precision.HIGHEST

    def attend(request):
        pages = (owner[request] * POOL + page_table[request]).astype(jnp.int32)
        page_keys = kv_pool[0, pages].reshape(span, HEADS, HEAD_DIM).astype(jnp.float32)
        page_values = kv_pool[1, pages].reshape(span, HEADS, HEAD_DIM).astype(jnp.float32)
        query_row = query[request].reshape(HEADS, HEAD_DIM).astype(jnp.float32)
        key_row = key_new[request].reshape(HEADS, HEAD_DIM).astype(jnp.float32)
        value_row = value_new[request].reshape(HEADS, HEAD_DIM).astype(jnp.float32)
        scores = jnp.einsum('hd,shd->hs', query_row, page_keys, precision=highest) * score_scale
        position_ok = (jnp.arange(span, dtype=jnp.int32) < lengths[request])[None, :]
        scores = jnp.where(position_ok, scores, -jnp.inf)
        self_score = lax.optimization_barrier(jnp.sum(query_row * key_row, axis=-1)) * score_scale
        top = jnp.maximum(lax.optimization_barrier(jnp.max(scores, axis=1)), self_score)
        weights = jnp.where(position_ok, jnp.exp(scores - top[:, None]), 0.0)
        self_weight = jnp.exp(self_score - top)
        denom = lax.optimization_barrier(jnp.sum(weights, axis=1)) + self_weight
        packed = weights.astype(jnp.bfloat16).astype(jnp.float32)
        numer = jnp.einsum('hs,shd->hd', packed, page_values, precision=highest)
        numer = numer + self_weight.astype(jnp.bfloat16).astype(jnp.float32)[:, None] * value_row
        return (numer / denom[:, None]).reshape(-1).astype(jnp.bfloat16)
    attn = lax.map(attend, jnp.arange(REQS, dtype=jnp.int32))
    projected = jnp.dot(attn, out_weight, preferred_element_type=jnp.float32)
    stream = (resid.astype(jnp.float32) + projected + out_bias.astype(jnp.float32)[None, :]).astype(jnp.bfloat16)
    stream_f = stream.astype(jnp.float32)
    mean = lax.optimization_barrier(jnp.mean(stream_f, axis=1, keepdims=True))
    var = lax.optimization_barrier(jnp.mean((stream_f - mean) ** 2, axis=1, keepdims=True))
    normed = ((stream_f - mean) * lax.rsqrt(var + 1e-05) * norm_gain.astype(jnp.float32)[None, :] + norm_bias.astype(jnp.float32)[None, :]).astype(jnp.bfloat16)
    hidden_in = jnp.dot(normed, up_weight_t.T, preferred_element_type=jnp.float32) + up_bias.astype(jnp.float32)[None, :]
    activated = jax.nn.gelu(hidden_in, approximate=False).astype(jnp.bfloat16)
    feed = jnp.dot(activated, down_weight, preferred_element_type=jnp.float32) + down_bias.astype(jnp.float32)[None, :]
    combined = stream_f + feed
    return combined[order].astype(jnp.bfloat16)
```

```python
import functools
import math

import jax
import jax.numpy as jnp
from jax import lax
from jax.experimental import pallas as pl
from jax.experimental.pallas import tpu as pltpu
from jax.sharding import PartitionSpec as P

HD = 128
EPS = 1e-05
F32 = jnp.float32
BF16 = jnp.bfloat16
NEG = -1e30


def layer_kernel(
    dims,
    meta_ref,
    table_ref,
    vec_ref,
    q_ref,
    k_ref,
    v_ref,
    res_ref,
    kv_hbm,
    ow_hbm,
    up_hbm,
    dw_hbm,
    out_ref,
    kv,
    ow,
    up,
    rhs,
    g0,
    g1,
    p0,
    r0,
    p1,
    r1,
    a0,
    a1,
    part,
    stream,
    nbuf,
    x32,
    xbuf,
    hbuf,
    onehot,
    place,
    lhs,
    fsend,
    frecv,
    ysend,
    yrecv,
    zsend,
    zrecv,
    local_sem,
    zq_s,
    zq_r,
    zv_s,
    zv_r,
    pq_s,
    pq_r,
    pv_s,
    pv_r,
    pt_s,
    pt_r,
    ng_s,
    ng_r,
    yg_s,
    yg_r,
    cg_s,
    cg_r,
    hd_s,
    hd_r,
    fc_s,
    fc_r,
    fy_s,
    fy_r,
    fz_s,
    fz_r,
):
    Z, Y, C, T, W, K = dims
    PL = Y * C
    R = Z * PL * K
    H = W // HD
    D = W * T
    ZK = Z * K
    FL = up.shape[0]
    me = lax.axis_index("req")
    t = lax.axis_index("tp")
    core = lax.rem(me, C)
    y = lax.rem(me // C, Y)
    z = me // PL
    pid = lax.rem(me, PL)

    def z_peer(d):
        other = lax.rem(z + d, Z)
        return other, {"req": other * PL + pid}

    def plane_peer(d):
        other = lax.rem(pid + d, PL)
        return other, {"req": z * PL + other}

    def y_peer(d):
        other = lax.rem(y + d, Y)
        return other, {"req": z * PL + other * C + core}

    def tp_peer(d):
        other = lax.rem(t + d, T)
        return other, {"tp": other}

    core_peer = {"req": z * PL + y * C + (1 - core)}

    def send(src, dst, ssem, rsem, device):
        copy = pltpu.make_async_remote_copy(
            src_ref=src,
            dst_ref=dst,
            send_sem=ssem,
            recv_sem=rsem,
            device_id=device,
            device_id_type=pl.DeviceIdType.MESH,
        )
        copy.start()

    def drain(ref, sem):
        pltpu.make_async_copy(ref, ref, sem).wait()

    def each(count, body):
        def step(d, carry):
            body(d)
            return carry

        lax.fori_loop(1, count, step, 0)

    barrier = pltpu.get_barrier_semaphore()

    def greet(peer):
        def body(d):
            pl.semaphore_signal(
                barrier, inc=1, device_id=peer(d)[1], device_id_type=pl.DeviceIdType.MESH
            )

        return body

    each(Z, greet(z_peer))
    each(PL, greet(plane_peer))
    each(T, greet(tp_peer))

    loads = [
        pltpu.make_async_copy(kv_hbm, kv, local_sem.at[0]),
        pltpu.make_async_copy(ow_hbm, ow, local_sem.at[1]),
        pltpu.make_async_copy(up_hbm, up, local_sem.at[2]),
        pltpu.make_async_copy(dw_hbm, rhs.at[pl.ds(0, FL)], local_sem.at[3]),
    ]
    for load in loads:
        load.start()

    scale = 1.0 / math.sqrt(HD)
    product = q_ref[...].astype(F32) * k_ref[...].astype(F32)
    lane = lax.broadcasted_iota(jnp.int32, (K, HD), 1)
    packed = jnp.zeros((K, HD), F32)
    for h in range(H):
        s = jnp.sum(product[:, h * HD : (h + 1) * HD], axis=1, keepdims=True) * scale
        high = s.astype(BF16).astype(F32)
        mid = (s - high).astype(BF16).astype(F32)
        low = (s - high - mid).astype(BF16).astype(F32)
        packed = jnp.where(lane == h, high, packed)
        packed = jnp.where(lane == H + h, mid, packed)
        packed = jnp.where(lane == 2 * H + h, low, packed)
    g0[z, :, 0:W] = q_ref[...]
    g0[z, :, W : W + HD] = packed.astype(BF16)
    g1[z, :, 0:W] = v_ref[...]
    g1[z, :, W : 2 * W] = res_ref[...]

    pl.semaphore_wait(barrier, (Z - 1) + (PL - 1) + (T - 1))

    each(Z, lambda d: send(g0.at[z], g0.at[z], zq_s, zq_r, z_peer(d)[1]))
    each(Z, lambda d: send(g1.at[z], g1.at[z], zv_s, zv_r, z_peer(d)[1]))

    len_row = meta_ref[0:1, :]
    owner_row = meta_ref[1:2, :]
    order_row = meta_ref[2:3, :]
    base_row = meta_ref[3:4, :]
    sub_i = lax.broadcasted_iota(jnp.int32, (R, R), 0)
    lane_i = lax.broadcasted_iota(jnp.int32, (R, R), 1)
    lane_f = lane_i.astype(F32)

    def column(row, index):
        return jnp.sum(jnp.where(lane_f == index, row, 0.0), axis=1, keepdims=True)

    iota_col = lax.broadcasted_iota(jnp.int32, (R, 1), 0)
    owner_col = column(owner_row, iota_col.astype(F32))
    earlier = jnp.where((owner_col == owner_row) & (sub_i < lane_i), 1.0, 0.0)
    rank_row = jnp.sum(earlier, axis=0, keepdims=True)

    kap = lax.broadcasted_iota(jnp.int32, (R, ZK), 1)
    kap_request = (kap // K) * (PL * K) + pid * K + kap % K
    pick = jnp.where(
        lax.broadcasted_iota(jnp.int32, (R, ZK), 0) == kap_request, 1.0, 0.0
    ).astype(BF16)
    sub8 = lax.broadcasted_iota(jnp.int32, (8, R), 0)
    pair = jnp.where(sub8 == 0, owner_row, jnp.where(sub8 == 1, rank_row, 0.0)).astype(BF16)
    picked = jnp.dot(pair, pick, preferred_element_type=F32)
    target = picked[0:1, :] * K + picked[1:2, :] - (z * (PL * K)).astype(F32)
    sort = jnp.where(
        lax.broadcasted_iota(jnp.int32, (PL * K, ZK), 0).astype(F32) == target, 1.0, 0.0
    ).astype(BF16)

    def to_plane(source, flat, sendbuf, recvbuf, zs, zr, ps, pr):
        drain(source.at[pl.ds(0, Z - 1)], zr)
        for s in range(Z):
            flat[s * K : (s + 1) * K, :] = source[s].astype(F32)
        rows = jnp.dot(sort, flat[...].astype(BF16), preferred_element_type=F32)
        for d in range(PL):
            sendbuf[d] = rows[d * K : (d + 1) * K, :].astype(BF16)
        recvbuf[pid] = sendbuf[pid]

        def body(d):
            other, device = plane_peer(d)
            send(sendbuf.at[other], recvbuf.at[pid], ps, pr, device)

        each(PL, body)
        drain(source.at[pl.ds(0, Z - 1)], zs)

    def from_plane(recvbuf, pr):
        drain(recvbuf.at[pl.ds(0, PL - 1)], pr)
        total = recvbuf[0].astype(F32)
        for s in range(1, PL):
            total = total + recvbuf[s].astype(F32)
        return total

    to_plane(g0, a0, p0, r0, zq_s, zq_r, pq_s, pq_r)

    mine = (owner_row == me.astype(F32)) & (
        rank_row == lax.broadcasted_iota(jnp.int32, (8, R), 0).astype(F32)
    )
    mine_f = jnp.where(mine, 1.0, 0.0)
    own_len = jnp.sum(mine_f * len_row, axis=1, keepdims=True)[0:K]
    own_table = jnp.dot(
        mine_f.astype(BF16), table_ref[...].astype(F32).astype(BF16), preferred_element_type=F32
    )[0:K]
    tokens = kv.shape[1]
    page_len = 32
    token = lax.broadcasted_iota(jnp.int32, (1, tokens), 1)
    page = (token // page_len).astype(F32)
    offset = (token % page_len).astype(F32)
    len_hk = jnp.concatenate([own_len] * H, axis=0)
    table_hk = jnp.concatenate([own_table] * H, axis=0)
    valid = jnp.zeros((H * K, tokens), F32)
    for j in range(table_ref.shape[1]):
        hit = (table_hk[:, j : j + 1] == page) & (offset + float(j * page_len) < len_hk)
        valid = jnp.where(hit, 1.0, valid)
    valid = valid > 0.5

    to_plane(g1, a1, p1, r1, zv_s, zv_r, pv_s, pv_r)

    own0 = from_plane(r0, pq_r)
    q_own = own0[:, 0:W]
    head_of_row = lax.broadcasted_iota(jnp.int32, (H * K, W), 0) // K
    head_of_lane = lax.broadcasted_iota(jnp.int32, (H * K, W), 1) // HD
    q_block = jnp.where(
        head_of_row == head_of_lane, jnp.concatenate([q_own] * H, axis=0), 0.0
    ).astype(BF16)
    self_col = jnp.concatenate(
        [
            own0[:, W + h : W + h + 1]
            + own0[:, W + H + h : W + H + h + 1]
            + own0[:, W + 2 * H + h : W + 2 * H + h + 1]
            for h in range(H)
        ],
        axis=0,
    )
    loads[0].wait()
    scores = (
        lax.dot_general(q_block, kv[0], (((1,), (1,)), ((), ())), preferred_element_type=F32)
        * scale
    )
    scores = jnp.where(valid, scores, NEG)
    top = jnp.maximum(jnp.max(scores, axis=1, keepdims=True), self_col)
    weights = jnp.where(valid, jnp.exp(scores - top), 0.0)
    self_weight = jnp.exp(self_col - top)
    total = jnp.sum(weights, axis=1, keepdims=True) + self_weight
    wide = jnp.dot(weights.astype(BF16), kv[1], preferred_element_type=F32)
    wide = jnp.where(head_of_row == head_of_lane, wide, 0.0)
    numer = wide[:, 0:HD]
    for h in range(1, H):
        numer = numer + wide[:, h * HD : (h + 1) * HD]

    own1 = from_plane(r1, pv_r)
    v_fold = jnp.concatenate([own1[:, h * HD : (h + 1) * HD] for h in range(H)], axis=0)
    numer = numer + self_weight.astype(BF16).astype(F32) * v_fold
    attn_fold = numer / total
    attn = jnp.concatenate([attn_fold[h * K : (h + 1) * K, :] for h in range(H)], axis=1).astype(
        BF16
    )

    loads[1].wait()
    part[t] = jnp.dot(attn, ow[...], preferred_element_type=F32)
    here = pl.ds(pl.multiple_of(t * W, W), W)
    part[t, :, here] = part[t, :, here] + (own1[:, W : 2 * W] + vec_ref[0:1, :])
    each(T, lambda d: send(part.at[t], part.at[t], pt_s, pt_r, tp_peer(d)[1]))
    drain(part.at[pl.ds(0, T - 1)], pt_r)
    summed = part[0]
    for s in range(1, T):
        summed = summed + part[s]
    rows_f = summed.astype(BF16).astype(F32)
    mean = jnp.sum(rows_f, axis=1, keepdims=True) * (1.0 / D)
    centred = rows_f - mean
    var = jnp.sum(centred * centred, axis=1, keepdims=True) * (1.0 / D)
    inverse = lax.rsqrt(var + EPS)
    stream[...] = rows_f
    mine_f32 = stream[:, here]
    nbuf[z] = ((mine_f32 - mean) * inverse * vec_ref[1:2, :] + vec_ref[2:3, :]).astype(BF16)

    each(Z, lambda d: send(nbuf.at[z], nbuf.at[z], ng_s, ng_r, z_peer(d)[1]))

    place_i = lax.broadcasted_iota(jnp.int32, (R, 1), 0)
    place_k = place_i % K
    place_z = (place_i // K) % Z
    place_y = (place_i // ZK) % Y
    place_c = place_i // (ZK * Y)
    natural = ((place_z * Y + place_y) * C + place_c) * K + place_k
    request = column(order_row, natural.astype(F32))
    slot = column(base_row + rank_row, request)
    onehot[...] = jnp.where(lane_f == slot, 1.0, 0.0).astype(BF16)
    my_base = (core * (Y * ZK) + y * ZK + z * K).astype(F32)
    lane_p = lax.broadcasted_iota(jnp.int32, (R, 2 * FL), 1)
    place[...] = jnp.where(
        (slot == my_base + (lane_p - FL).astype(F32)) & (lane_p >= FL) & (lane_p < FL + K),
        1.0,
        0.0,
    )
    rhs[FL : 2 * FL, :] = jnp.concatenate(
        [mine_f32, jnp.zeros((FL - K, W), F32)], axis=0
    ).astype(BF16)
    drain(p0.at[pl.ds(0, PL - 1)], pq_s)
    drain(p1.at[pl.ds(0, PL - 1)], pv_s)
    drain(part.at[pl.ds(0, T - 1)], pt_s)

    drain(nbuf.at[pl.ds(0, Z - 1)], ng_r)
    for s in range(Z):
        x32[s * K : (s + 1) * K, :] = nbuf[s].astype(F32)
    xbuf[core, y] = x32[...].astype(BF16)
    for d in range(1, Y):
        other, device = y_peer(d)
        send(xbuf.at[core, y], xbuf.at[core, y], yg_s.at[d], yg_r.at[y], device)
    send(xbuf.at[core, y], xbuf.at[core, y], cg_s.at[0], cg_r.at[y], core_peer)
    for d in range(1, Y):
        other, device = y_peer(d)
        drain(xbuf.at[core, other], yg_r.at[other])
        send(xbuf.at[core, other], xbuf.at[core, other], cg_s.at[d], cg_r.at[other], core_peer)
    for s in range(Y):
        drain(xbuf.at[1 - core, s], cg_r.at[s])

    loads[2].wait()
    hidden = lax.dot_general(
        up[...], xbuf[...].reshape(R, W), (((1,), (1,)), ((), ())), preferred_element_type=F32
    )
    hbuf[t] = hidden.astype(BF16)
    each(T, lambda d: send(hbuf.at[t], hbuf.at[t], hd_s, hd_r, tp_peer(d)[1]))
    up_bias = jnp.sum(
        jnp.where(
            lax.broadcasted_iota(jnp.int32, (FL, FL), 0)
            == lax.broadcasted_iota(jnp.int32, (FL, FL), 1),
            vec_ref[4:5, 0:FL],
            0.0,
        ),
        axis=1,
        keepdims=True,
    )
    drain(nbuf.at[pl.ds(0, Z - 1)], ng_s)
    for d in range(1, Y):
        drain(xbuf.at[core, y], yg_s.at[d])
    for d in range(Y):
        drain(xbuf.at[core, y], cg_s.at[d])
    drain(hbuf.at[pl.ds(0, T - 1)], hd_r)
    before = hbuf[0].astype(F32)
    for s in range(1, T):
        before = before + hbuf[s].astype(F32)
    before = before + up_bias
    active = 0.5 * before * (1.0 + lax.erf(before * math.sqrt(0.5)))
    active = jnp.concatenate([active, jnp.zeros((FL, R), F32)], axis=0).astype(BF16)
    lhs[...] = (
        lax.dot_general(onehot[...], active, (((1,), (1,)), ((), ())), preferred_element_type=F32)
        + place[...]
    ).astype(BF16)
    loads[3].wait()

    def feed_rows(half, block):
        start = pl.multiple_of(half * (Y * ZK) + block * ZK, ZK)
        return jnp.dot(lhs[pl.ds(start, ZK), :], rhs[...], preferred_element_type=F32)

    for d in range(1, Y + 1):
        block = lax.rem(y + d, Y)
        fsend[block] = feed_rows(1 - core, block).astype(BF16)
        send(fsend.at[block], frecv.at[block], fc_s.at[block], fc_r.at[block], core_peer)
    for d in range(1, Y):
        block, device = y_peer(d)
        mine_half = feed_rows(core, block)
        drain(frecv.at[block], fc_r.at[block])
        ysend[block] = (mine_half + frecv[block].astype(F32)).astype(BF16)
        send(ysend.at[block], yrecv.at[y], fy_s.at[block], fy_r.at[y], device)
    mine_half = feed_rows(core, y)
    drain(frecv.at[y], fc_r.at[y])
    rows = mine_half + frecv[y].astype(F32)
    for d in range(1, Y):
        other, _ = y_peer(d)
        drain(yrecv.at[other], fy_r.at[other])
        rows = rows + yrecv[other].astype(F32)
    for s in range(Z):
        zsend[s] = rows[s * K : (s + 1) * K, :].astype(BF16)
    zrecv[z] = zsend[z]

    def scatter(d):
        other, device = z_peer(d)
        send(zsend.at[other], zrecv.at[z], fz_s, fz_r, device)

    each(Z, scatter)
    drain(hbuf.at[pl.ds(0, T - 1)], hd_s)
    for s in range(Y):
        drain(fsend.at[s], fc_s.at[s])
    for d in range(1, Y):
        other, _ = y_peer(d)
        drain(ysend.at[other], fy_s.at[other])
    drain(zrecv.at[pl.ds(0, Z - 1)], fz_r)
    final = zrecv[0].astype(F32)
    for s in range(1, Z):
        final = final + zrecv[s].astype(F32)
    out_ref[...] = (final + vec_ref[3:4, :]).astype(BF16)
    drain(zsend.at[pl.ds(0, Z - 1)], fz_s)


def chip_grid(devices):
    cores = 2
    along_y = 4 if devices >= 32 else 2
    return devices // (along_y * cores), along_y, cores


def per_device(
    query,
    key_new,
    value_new,
    resid,
    lengths,
    owner,
    page_table,
    kv_pool,
    out_weight,
    out_bias,
    norm_gain,
    norm_bias,
    up_weight_t,
    up_bias,
    down_weight,
    down_bias,
    order,
):
    K, W = query.shape
    devices = lax.axis_size("req")
    T = lax.axis_size("tp")
    Z, Y, C = chip_grid(devices)
    PL = Y * C
    R = devices * K
    D = W * T
    FL = up_weight_t.shape[0]
    pages, page_len = kv_pool.shape[1], kv_pool.shape[2]
    tokens = pages * page_len
    base = (owner % C) * (Y * Z * K) + ((owner // C) % Y) * (Z * K) + (owner // PL) * K
    meta = jnp.stack([lengths, owner, order, base]).astype(F32)
    vec = jnp.stack(
        [out_bias, norm_gain, norm_bias, down_bias, jnp.pad(up_bias, (0, W - FL))]
    ).astype(F32)
    vmem = pl.BlockSpec(memory_space=pltpu.VMEM)
    anywhere = pl.BlockSpec(memory_space=pl.ANY)
    dma = pltpu.SemaphoreType.DMA
    return pl.pallas_call(
        functools.partial(layer_kernel, (Z, Y, C, T, W, K)),
        out_shape=jax.ShapeDtypeStruct((K, W), BF16),
        in_specs=[vmem] * 7 + [anywhere] * 4,
        out_specs=vmem,
        scratch_shapes=[
            pltpu.VMEM((2, tokens, W), BF16),
            pltpu.VMEM((W, D), BF16),
            pltpu.VMEM((FL, W), BF16),
            pltpu.VMEM((2 * FL, W), BF16),
            pltpu.VMEM((Z, K, W + HD), BF16),
            pltpu.VMEM((Z, K, 2 * W), BF16),
            pltpu.VMEM((PL, K, W + HD), BF16),
            pltpu.VMEM((PL, K, W + HD), BF16),
            pltpu.VMEM((PL, K, 2 * W), BF16),
            pltpu.VMEM((PL, K, 2 * W), BF16),
            pltpu.VMEM((Z * K, W + HD), F32),
            pltpu.VMEM((Z * K, 2 * W), F32),
            pltpu.VMEM((T, K, D), F32),
            pltpu.VMEM((K, D), F32),
            pltpu.VMEM((Z, K, W), BF16),
            pltpu.VMEM((Z * K, W), F32),
            pltpu.VMEM((C, Y, Z * K, W), BF16),
            pltpu.VMEM((T, FL, R), BF16),
            pltpu.VMEM((R, R), BF16),
            pltpu.VMEM((R, 2 * FL), F32),
            pltpu.VMEM((R, 2 * FL), BF16),
            pltpu.VMEM((Y, Z * K, W), BF16),
            pltpu.VMEM((Y, Z * K, W), BF16),
            pltpu.VMEM((Y, Z * K, W), BF16),
            pltpu.VMEM((Y, Z * K, W), BF16),
            pltpu.VMEM((Z, K, W), BF16),
            pltpu.VMEM((Z, K, W), BF16),
            dma((4,)),
        ]
        + [dma(())] * 12
        + [dma((Y,))] * 4
        + [dma(())] * 2
        + [dma((Y,))] * 4
        + [dma(())] * 2,
        compiler_params=pltpu.CompilerParams(
            collective_id=0, has_side_effects=True, vmem_limit_bytes=48 * 1024 * 1024
        ),
    )(
        meta,
        page_table,
        vec,
        query,
        key_new,
        value_new,
        resid,
        kv_pool.reshape(2, tokens, W),
        out_weight,
        up_weight_t,
        down_weight,
    )


def solution(mesh):
    in_specs = (
        P("req", "tp"),
        P("req", "tp"),
        P("req", "tp"),
        P("req", "tp"),
        P(),
        P(),
        P(),
        P(None, "req", None, "tp"),
        P("tp", None),
        P("tp"),
        P("tp"),
        P("tp"),
        P("req", "tp"),
        P("req"),
        P("req", "tp"),
        P("tp"),
        P(),
    )
    return jax.shard_map(
        per_device, mesh=mesh, in_specs=in_specs, out_specs=P("req", "tp"), check_vma=False
    )
```

```python
import functools
import math

import jax
import jax.numpy as jnp
from jax import lax
from jax.experimental import pallas as pl
from jax.experimental.pallas import tpu as pltpu
from jax.sharding import PartitionSpec as P

HD = 128
EPS = 1e-05
F32 = jnp.float32
BF16 = jnp.bfloat16
NEG = -1e30


def over(x, n):
    return lax.shift_right_logical(x, n.bit_length() - 1)


def within(x, n):
    return x & (n - 1)


def iota(shape, dim):
    return lax.broadcasted_iota(jnp.int32, shape, dim)


def hot(mask):
    return jnp.where(mask, 1.0, 0.0).astype(BF16)


def layer_kernel(
    dims,
    q_hbm,
    k_hbm,
    v_hbm,
    res_hbm,
    owner_hbm,
    order_hbm,
    len_hbm,
    table_hbm,
    kv_hbm,
    ow_hbm,
    up_hbm,
    dw_hbm,
    ob_hbm,
    ng_hbm,
    nb_hbm,
    ub_hbm,
    db_hbm,
    out_ref,
    q_ref,
    k_ref,
    meta_ref,
    table_ref,
    ob_ref,
    ng_ref,
    nb_ref,
    ub_ref,
    db_ref,
    kv,
    ow,
    wts,
    g0,
    g1,
    p0,
    r0,
    p1,
    r1,
    a0,
    a1,
    part,
    stream,
    nbuf,
    x32,
    hbuf,
    abuf,
    zsend,
    zrecv,
    local_sem,
    zq_s,
    zq_r,
    zv_s,
    zv_r,
    pq_s,
    pq_r,
    pv_s,
    pv_r,
    pt_s,
    pt_r,
    ng_s,
    ng_r,
    hd_s,
    hd_r,
    wy_s,
    wy_r,
    wc_s,
    wc_r,
    ay_s,
    ay_r,
    ac_s,
    ac_r,
    fz_s,
    fz_r,
):
    Z, Y, C, T, W, K = dims
    PL = Y * C
    R = Z * PL * K
    H = W // HD
    D = W * T
    ZK = Z * K
    FL = up_hbm.shape[0]
    BLK = ZK + 8
    me = lax.axis_index("req")
    t = lax.axis_index("tp")
    core = lax.rem(me, C)
    y = lax.rem(me // C, Y)
    z = me // PL
    pid = lax.rem(me, PL)

    def far_first(i, n):
        return n // 2 + (i // 2) * (1 - 2 * (i % 2))

    def z_peer(i):
        other = lax.rem(z + far_first(i, Z), Z)
        return other, {"req": other * PL + pid}

    plane_steps = sorted(
        [(a, b) for a in range(Y) for b in range(C) if a or b],
        key=lambda step: -min(step[0], Y - step[0]),
    )

    def plane_peer(step):
        other = lax.rem(y + step[0], Y) * C + lax.rem(core + step[1], C)
        return other, {"req": z * PL + other}

    def y_peer(i):
        other = lax.rem(y + far_first(i, Y), Y)
        return other, {"req": z * PL + other * C + core}

    def tp_peer(i):
        other = lax.rem(t + far_first(i, T), T)
        return other, {"tp": other}

    core_peer = {"req": z * PL + y * C + (1 - core)}

    def send(src, dst, ssem, rsem, device):
        copy = pltpu.make_async_remote_copy(
            src_ref=src,
            dst_ref=dst,
            send_sem=ssem,
            recv_sem=rsem,
            device_id=device,
            device_id_type=pl.DeviceIdType.MESH,
        )
        copy.start()

    def drain(ref, sem):
        pltpu.make_async_copy(ref, ref, sem).wait()

    def each(count, body):
        def step(d, carry):
            body(d)
            return carry

        lax.fori_loop(1, count, step, 0)

    pairs = [
        (q_hbm, q_ref),
        (k_hbm, k_ref),
        (q_hbm, g0.at[z, :, pl.ds(0, W)]),
        (v_hbm, g1.at[z, :, pl.ds(0, W)]),
        (res_hbm, g1.at[z, :, pl.ds(W, W)]),
        (owner_hbm, meta_ref.at[0]),
        (order_hbm, meta_ref.at[1]),
        (len_hbm, meta_ref.at[2]),
        (table_hbm, table_ref),
        (kv_hbm, kv),
        (ow_hbm, ow),
        (up_hbm, wts.at[pid, pl.ds(0, FL)]),
        (dw_hbm, wts.at[pid, pl.ds(FL, FL)]),
        (ob_hbm, ob_ref),
        (ng_hbm, ng_ref),
        (nb_hbm, nb_ref),
        (ub_hbm, ub_ref),
        (db_hbm, db_ref),
    ]
    loads = [pltpu.make_async_copy(a, b, local_sem.at[i]) for i, (a, b) in enumerate(pairs)]

    def vector(ref):
        return ref[...].astype(F32).reshape(1, ref.shape[0])

    barrier = pltpu.get_barrier_semaphore()

    def greet(peer):
        def body(d):
            pl.semaphore_signal(
                barrier, inc=1, device_id=peer(d)[1], device_id_type=pl.DeviceIdType.MESH
            )

        return body

    each(Z, greet(z_peer))
    for step in plane_steps:
        greet(plane_peer)(step)
    each(T, greet(tp_peer))

    for load in loads:
        load.start()

    scale = 1.0 / math.sqrt(HD)
    loads[0].wait()
    loads[1].wait()
    product = q_ref[...].astype(F32) * k_ref[...].astype(F32)
    lane = lax.broadcasted_iota(jnp.int32, (K, HD), 1)
    packed = jnp.zeros((K, HD), F32)
    for h in range(H):
        s = jnp.sum(product[:, h * HD : (h + 1) * HD], axis=1, keepdims=True) * scale
        high = s.astype(BF16).astype(F32)
        mid = (s - high).astype(BF16).astype(F32)
        low = (s - high - mid).astype(BF16).astype(F32)
        packed = jnp.where(lane == h, high, packed)
        packed = jnp.where(lane == H + h, mid, packed)
        packed = jnp.where(lane == 2 * H + h, low, packed)
    g0[z, :, W : W + HD] = packed.astype(BF16)

    for load in loads[2:5]:
        load.wait()
    pl.semaphore_wait(barrier, (Z - 1) + (PL - 1) + (T - 1))

    each(Z, lambda d: send(g0.at[z], g0.at[z], zq_s, zq_r, z_peer(d)[1]))
    each(Z, lambda d: send(g1.at[z], g1.at[z], zv_s, zv_r, z_peer(d)[1]))

    for load in [loads[11], loads[12], loads[16]]:
        load.wait()
    spread = hot(iota((FL, W), 1) == pid * FL + iota((FL, W), 0))
    bias8 = jnp.where(iota((8, FL), 0) == 0, vector(ub_ref), 0.0)
    wts[pid, 2 * FL : 2 * FL + 8, :] = jnp.dot(
        bias8.astype(BF16), spread, preferred_element_type=F32
    ).astype(BF16)
    for i in range(1, Y):
        send(wts.at[pid], wts.at[pid], wy_s.at[i], wy_r.at[y], y_peer(i)[1])
    send(wts.at[pid], wts.at[pid], wc_s.at[0], wc_r.at[y], core_peer)

    for load in loads[5:9]:
        load.wait()
    owner_i = meta_ref[0]
    owner_row = owner_i.astype(F32)
    order_i = meta_ref[1]
    len_row = meta_ref[2].astype(F32)

    owners = Z * PL
    lanes = min(R, HD)
    earlier = hot(iota((lanes, lanes), 0) < iota((lanes, lanes), 1))
    ones = jnp.ones((lanes, lanes), BF16)
    before = None
    ranks = []
    for b in range(R // lanes):
        mask = iota((owners, lanes), 0) == owner_i[:, b * lanes : (b + 1) * lanes]
        mask_f = jnp.where(mask, 1.0, 0.0)
        count = jnp.dot(mask_f.astype(BF16), earlier, preferred_element_type=F32)
        if before is not None:
            count = count + jnp.dot(before.astype(BF16), ones, preferred_element_type=F32)
        ranks.append(jnp.sum(mask_f * count, axis=0, keepdims=True))
        before = mask_f if before is None else before + mask_f
    rank_row = jnp.concatenate(ranks, axis=1)

    KL = max(ZK, HD)
    kap = iota((1, KL), 1)
    kap_request = over(kap, K) * (PL * K) + pid * K + within(kap, K)
    pick = hot(iota((R, KL), 0) == kap_request)
    sub8 = iota((8, R), 0)

    def stacked(*rows):
        total = jnp.zeros((8, R), F32)
        for i, row in enumerate(rows):
            total = jnp.where(sub8 == i, row.astype(F32), total)
        return total.astype(BF16)

    picked = jnp.dot(
        stacked(owner_row, rank_row, over(order_i, 16), within(order_i, 16)),
        pick,
        preferred_element_type=F32,
    )
    target = picked[0:1, 0:ZK] * K + picked[1:2, 0:ZK] - (z * (PL * K)).astype(F32)
    sort = hot(iota((PL * K, ZK), 0).astype(F32) == target)
    out_request = (picked[2:3, :] * 16.0 + picked[3:4, :]).astype(jnp.int32)

    def to_plane(source, flat, sendbuf, recvbuf, zs, zr, ps, pr):
        drain(source.at[pl.ds(0, Z - 1)], zr)
        for s in range(Z):
            flat[s * K : (s + 1) * K, :] = source[s].astype(F32)
        rows = jnp.dot(sort, flat[...].astype(BF16), preferred_element_type=F32)
        for d in range(PL):
            sendbuf[d] = rows[d * K : (d + 1) * K, :].astype(BF16)
        recvbuf[pid] = sendbuf[pid]

        def body(step):
            other, device = plane_peer(step)
            send(sendbuf.at[other], recvbuf.at[pid], ps, pr, device)

        for step in plane_steps:
            body(step)
        drain(source.at[pl.ds(0, Z - 1)], zs)

    def from_plane(recvbuf, pr):
        drain(recvbuf.at[pl.ds(0, PL - 1)], pr)
        total = recvbuf[0].astype(F32)
        for s in range(1, PL):
            total = total + recvbuf[s].astype(F32)
        return total

    to_plane(g0, a0, p0, r0, zq_s, zq_r, pq_s, pq_r)
    for i in range(1, Y):
        other, _ = y_peer(i)
        arrived = wts.at[other * C + core]
        drain(arrived, wy_r.at[other])
        send(arrived, arrived, wc_s.at[i], wc_r.at[other], core_peer)

    mine = (owner_row == me.astype(F32)) & (
        rank_row == sub8.astype(F32)
    )
    mine_f = jnp.where(mine, 1.0, 0.0)
    own_len = jnp.sum(mine_f * len_row, axis=1, keepdims=True)[0:K]
    own_table = lax.dot_general(
        mine_f.astype(BF16),
        table_ref[...].astype(F32).astype(BF16),
        (((1,), (1,)), ((), ())),
        preferred_element_type=F32,
    )[0:K]
    tokens = kv.shape[1]
    page_len = 32
    token = lax.broadcasted_iota(jnp.int32, (1, tokens), 1)
    page = over(token, page_len).astype(F32)
    offset = within(token, page_len).astype(F32)
    len_hk = jnp.concatenate([own_len] * H, axis=0)
    table_hk = jnp.concatenate([own_table] * H, axis=0)
    valid = jnp.zeros((H * K, tokens), F32)
    for j in range(table_ref.shape[0]):
        hit = (table_hk[:, j : j + 1] == page) & (offset + float(j * page_len) < len_hk)
        valid = jnp.where(hit, 1.0, valid)
    valid = valid > 0.5

    to_plane(g1, a1, p1, r1, zv_s, zv_r, pv_s, pv_r)

    own0 = from_plane(r0, pq_r)
    q_own = own0[:, 0:W]
    head_of_row = over(iota((H * K, W), 0), K)
    head_of_lane = over(iota((H * K, W), 1), HD)
    q_block = jnp.where(
        head_of_row == head_of_lane, jnp.concatenate([q_own] * H, axis=0), 0.0
    ).astype(BF16)
    self_col = jnp.concatenate(
        [
            own0[:, W + h : W + h + 1]
            + own0[:, W + H + h : W + H + h + 1]
            + own0[:, W + 2 * H + h : W + 2 * H + h + 1]
            for h in range(H)
        ],
        axis=0,
    )
    loads[9].wait()
    scores = (
        lax.dot_general(q_block, kv[0], (((1,), (1,)), ((), ())), preferred_element_type=F32)
        * scale
    )
    scores = jnp.where(valid, scores, NEG)
    top = jnp.maximum(jnp.max(scores, axis=1, keepdims=True), self_col)
    weights = jnp.where(valid, jnp.exp(scores - top), 0.0)
    self_weight = jnp.exp(self_col - top)
    total = jnp.sum(weights, axis=1, keepdims=True) + self_weight
    wide = jnp.dot(weights.astype(BF16), kv[1], preferred_element_type=F32)
    wide = jnp.where(head_of_row == head_of_lane, wide, 0.0)
    numer = wide[:, 0:HD]
    for h in range(1, H):
        numer = numer + wide[:, h * HD : (h + 1) * HD]

    own1 = from_plane(r1, pv_r)
    v_fold = jnp.concatenate([own1[:, h * HD : (h + 1) * HD] for h in range(H)], axis=0)
    numer = numer + self_weight.astype(BF16).astype(F32) * v_fold
    attn_fold = numer / total
    attn = jnp.concatenate([attn_fold[h * K : (h + 1) * K, :] for h in range(H)], axis=1).astype(
        BF16
    )

    loads[10].wait()
    for load in [loads[13], loads[14], loads[15], loads[17]]:
        load.wait()
    part[t] = jnp.dot(attn, ow[...], preferred_element_type=F32)
    here = pl.ds(pl.multiple_of(t * W, W), W)
    part[t, :, here] = part[t, :, here] + (own1[:, W : 2 * W] + vector(ob_ref))
    each(T, lambda d: send(part.at[t], part.at[t], pt_s, pt_r, tp_peer(d)[1]))
    drain(part.at[pl.ds(0, T - 1)], pt_r)
    summed = part[0]
    for s in range(1, T):
        summed = summed + part[s]
    rows_f = summed.astype(BF16).astype(F32)
    mean = jnp.sum(rows_f, axis=1, keepdims=True) * (1.0 / D)
    centred = rows_f - mean
    var = jnp.sum(centred * centred, axis=1, keepdims=True) * (1.0 / D)
    inverse = lax.rsqrt(var + EPS)
    stream[...] = rows_f
    mine_f32 = stream[:, here]
    nbuf[z] = ((mine_f32 - mean) * inverse * vector(ng_ref) + vector(nb_ref)).astype(BF16)

    each(Z, lambda d: send(nbuf.at[z], nbuf.at[z], ng_s, ng_r, z_peer(d)[1]))

    found = jnp.dot(
        stacked(owner_row, rank_row), hot(iota((R, KL), 0) == out_request), preferred_element_type=F32
    )
    home = found[0:1, :].astype(jnp.int32)
    block = (within(home, C) * Y + within(over(home, C), Y)) * BLK + found[1:2, :].astype(jnp.int32)
    row_at = block + over(home, PL) * K
    stream_at = jnp.where(over(home, PL) == z, block + ZK, -1)
    at8 = jnp.where(
        iota((8, KL), 0) == 0,
        row_at.astype(F32),
        stream_at.astype(F32),
    )
    at_col = jnp.transpose(at8)[0:ZK, :]
    lane_a = iota((ZK, PL * BLK), 1).astype(F32)
    choose = jnp.concatenate(
        [hot(lane_a == at_col[:, 0:1]), hot(lane_a == at_col[:, 1:2])], axis=0
    )
    abuf[core, y, ZK:BLK, :] = jnp.concatenate(
        [mine_f32, jnp.zeros((BLK - ZK - K, W), F32)], axis=0
    ).astype(BF16)
    drain(p0.at[pl.ds(0, PL - 1)], pq_s)
    drain(p1.at[pl.ds(0, PL - 1)], pv_s)
    drain(part.at[pl.ds(0, T - 1)], pt_s)

    drain(nbuf.at[pl.ds(0, Z - 1)], ng_r)
    for s in range(Z):
        x32[s * K : (s + 1) * K, :] = nbuf[s].astype(F32)
    for i in range(1, Y + 1):
        if i < Y:
            other, _ = y_peer(i)
            arrived = other * C + (1 - core)
        else:
            arrived = y * C + (1 - core)
            other = y
        drain(wts.at[arrived], wc_r.at[other])

    up = jnp.concatenate([wts[p, 0:FL, :] for p in range(PL)], axis=0)
    hidden = lax.dot_general(
        x32[...].astype(BF16), up, (((1,), (1,)), ((), ())), preferred_element_type=F32
    )
    hbuf[t] = hidden.astype(BF16)
    each(T, lambda d: send(hbuf.at[t], hbuf.at[t], hd_s, hd_r, tp_peer(d)[1]))
    up_bias = wts[0, 2 * FL : 2 * FL + 8, :].astype(F32)
    for p in range(1, PL):
        up_bias = up_bias + wts[p, 2 * FL : 2 * FL + 8, :].astype(F32)
    down = jnp.concatenate([wts[p, FL : 2 * FL, :] for p in range(PL)], axis=0)
    drain(nbuf.at[pl.ds(0, Z - 1)], ng_s)
    for i in range(1, Y):
        drain(wts.at[pid], wy_s.at[i])
    for i in range(Y):
        drain(wts.at[pid], wc_s.at[i])
    drain(hbuf.at[pl.ds(0, T - 1)], hd_r)
    before = hbuf[0].astype(F32)
    for s in range(1, T):
        before = before + hbuf[s].astype(F32)
    before = before + up_bias[0:1, 0 : PL * FL]
    active = 0.5 * before * (1.0 + lax.erf(before * math.sqrt(0.5)))
    abuf[core, y, 0:ZK, 0 : PL * FL] = active.astype(BF16)
    if PL * FL < W:
        abuf[core, y, 0:ZK, PL * FL : W] = jnp.zeros((ZK, W - PL * FL), BF16)

    for i in range(1, Y):
        send(abuf.at[core, y], abuf.at[core, y], ay_s.at[i], ay_r.at[y], y_peer(i)[1])
    send(abuf.at[core, y], abuf.at[core, y], ac_s.at[0], ac_r.at[y], core_peer)
    for i in range(Y - 1, 0, -1):
        other, _ = y_peer(i)
        drain(abuf.at[core, other], ay_r.at[other])
        send(abuf.at[core, other], abuf.at[core, other], ac_s.at[i], ac_r.at[other], core_peer)
    for s in range(Y):
        drain(abuf.at[1 - core, s], ac_r.at[s])

    gathered = jnp.concatenate([abuf[p // Y, p % Y] for p in range(PL)], axis=0)
    chosen = jnp.dot(choose, gathered, preferred_element_type=F32)
    rows = chosen[ZK : 2 * ZK, 0:W] + jnp.dot(
        chosen[0:ZK, 0 : PL * FL].astype(BF16), down, preferred_element_type=F32
    )

    for s in range(Z):
        zsend[s] = rows[s * K : (s + 1) * K, :].astype(BF16)
    zrecv[z] = zsend[z]

    def scatter(i):
        other, device = z_peer(i)
        send(zsend.at[other], zrecv.at[z], fz_s, fz_r, device)

    each(Z, scatter)
    drain(hbuf.at[pl.ds(0, T - 1)], hd_s)
    for i in range(1, Y):
        drain(abuf.at[core, y], ay_s.at[i])
    for i in range(Y):
        drain(abuf.at[core, y], ac_s.at[i])
    drain(zrecv.at[pl.ds(0, Z - 1)], fz_r)
    final = zrecv[0].astype(F32)
    for s in range(1, Z):
        final = final + zrecv[s].astype(F32)
    out_ref[...] = (final + vector(db_ref)).astype(BF16)
    drain(zsend.at[pl.ds(0, Z - 1)], fz_s)


def chip_grid(devices):
    cores = 2
    along_y = 4 if devices >= 32 else 2
    return devices // (along_y * cores), along_y, cores


def per_device(
    query,
    key_new,
    value_new,
    resid,
    lengths,
    owner,
    page_table,
    kv_pool,
    out_weight,
    out_bias,
    norm_gain,
    norm_bias,
    up_weight_t,
    up_bias,
    down_weight,
    down_bias,
    order,
):
    K, W = query.shape
    devices = lax.axis_size("req")
    T = lax.axis_size("tp")
    Z, Y, C = chip_grid(devices)
    PL = Y * C
    R = devices * K
    D = W * T
    FL = up_weight_t.shape[0]
    pages, page_len = kv_pool.shape[1], kv_pool.shape[2]
    tokens = pages * page_len
    vmem = pl.BlockSpec(memory_space=pltpu.VMEM)
    hbm = pl.BlockSpec(memory_space=pltpu.HBM)
    dma = pltpu.SemaphoreType.DMA
    return pl.pallas_call(
        functools.partial(layer_kernel, (Z, Y, C, T, W, K)),
        out_shape=jax.ShapeDtypeStruct((K, W), BF16),
        in_specs=[hbm] * 17,
        out_specs=vmem,
        scratch_shapes=[
            pltpu.VMEM((K, W), BF16),
            pltpu.VMEM((K, W), BF16),
            pltpu.VMEM((3, 1, R), jnp.int32),
            pltpu.VMEM((page_table.shape[1], R), jnp.int32),
            pltpu.VMEM((W,), BF16),
            pltpu.VMEM((W,), BF16),
            pltpu.VMEM((W,), BF16),
            pltpu.VMEM((FL,), BF16),
            pltpu.VMEM((W,), BF16),
            pltpu.VMEM((2, tokens, W), BF16),
            pltpu.VMEM((W, D), BF16),
            pltpu.VMEM((PL, 2 * FL + 8, W), BF16),
            pltpu.VMEM((Z, K, W + HD), BF16),
            pltpu.VMEM((Z, K, 2 * W), BF16),
            pltpu.VMEM((PL, K, W + HD), BF16),
            pltpu.VMEM((PL, K, W + HD), BF16),
            pltpu.VMEM((PL, K, 2 * W), BF16),
            pltpu.VMEM((PL, K, 2 * W), BF16),
            pltpu.VMEM((Z * K, W + HD), F32),
            pltpu.VMEM((Z * K, 2 * W), F32),
            pltpu.VMEM((T, K, D), F32),
            pltpu.VMEM((K, D), F32),
            pltpu.VMEM((Z, K, W), BF16),
            pltpu.VMEM((Z * K, W), F32),
            pltpu.VMEM((T, Z * K, PL * FL), BF16),
            pltpu.VMEM((C, Y, Z * K + 8, W), BF16),
            pltpu.VMEM((Z, K, W), BF16),
            pltpu.VMEM((Z, K, W), BF16),
            dma((18,)),
        ]
        + [dma(())] * 14
        + [dma((Y,))] * 8
        + [dma(())] * 2,
        compiler_params=pltpu.CompilerParams(
            collective_id=0, has_side_effects=True, vmem_limit_bytes=60 * 1024 * 1024
        ),
    )(
        query,
        key_new,
        value_new,
        resid,
        owner.reshape(1, R),
        order.reshape(1, R),
        lengths.reshape(1, R),
        page_table.T,
        kv_pool.reshape(2, tokens, W),
        out_weight,
        up_weight_t,
        down_weight,
        out_bias,
        norm_gain,
        norm_bias,
        up_bias,
        down_bias,
    )


def solution(mesh):
    in_specs = (
        P("req", "tp"),
        P("req", "tp"),
        P("req", "tp"),
        P("req", "tp"),
        P(),
        P(),
        P(),
        P(None, "req", None, "tp"),
        P("tp", None),
        P("tp"),
        P("tp"),
        P("tp"),
        P("req", "tp"),
        P("req"),
        P("req", "tp"),
        P("tp"),
        P(),
    )
    return jax.shard_map(
        per_device, mesh=mesh, in_specs=in_specs, out_specs=P("req", "tp"), check_vma=False
    )
```

```python
import functools
import math

import jax
import jax.numpy as jnp
from jax import lax
from jax.experimental import pallas as pl
from jax.experimental.pallas import tpu as pltpu
from jax.sharding import PartitionSpec as P

HD = 128
EPS = 1e-05
F32 = jnp.float32
BF16 = jnp.bfloat16
NEG = -1e30


def over(x, n):
    return lax.shift_right_logical(x, n.bit_length() - 1)


def within(x, n):
    return x & (n - 1)


def iota(shape, dim):
    return lax.broadcasted_iota(jnp.int32, shape, dim)


def hot(mask):
    return jnp.where(mask, 1.0, 0.0).astype(BF16)


def layer_kernel(
    dims,
    q_hbm,
    k_hbm,
    v_hbm,
    res_hbm,
    owner_hbm,
    order_hbm,
    len_hbm,
    table_hbm,
    kv_hbm,
    ow_hbm,
    up_hbm,
    dw_hbm,
    ob_hbm,
    ng_hbm,
    nb_hbm,
    ub_hbm,
    db_hbm,
    out_ref,
    q_ref,
    k_ref,
    meta_ref,
    table_ref,
    ob_ref,
    ng_ref,
    nb_ref,
    ub_ref,
    db_ref,
    kv,
    ow,
    wts,
    g0,
    g1,
    g2,
    p0,
    p1,
    p2,
    r0,
    r1,
    r2,
    a0,
    a1,
    a2,
    part,
    stream,
    nbuf,
    x32,
    hbuf,
    abuf,
    zsend,
    zrecv,
    local_sem,
    near_s,
    below_r,
    above_r,
    far_s,
    far_r,
    plane_s,
    plane_r,
    pt_s,
    pt_r,
    ng_s,
    ng_r,
    hd_s,
    hd_r,
    wy_s,
    wy_r,
    wc_s,
    wc_r,
    ay_s,
    ay_r,
    ac_s,
    ac_r,
    fz_s,
    fz_r,
):
    Z, Y, C, T, W, K = dims
    PL = Y * C
    R = Z * PL * K
    H = W // HD
    D = W * T
    ZK = Z * K
    FL = up_hbm.shape[0]
    BLK = ZK + 8
    MID = Z // 2
    REACH = Z // 4
    me = lax.axis_index("req")
    t = lax.axis_index("tp")
    core = lax.rem(me, C)
    y = lax.rem(me // C, Y)
    z = me // PL
    pid = lax.rem(me, PL)

    def far_first(i, n):
        return n // 2 + (i // 2) * (1 - 2 * (i % 2))

    def z_away(d):
        return {"req": lax.rem(z + d + Z, Z) * PL + pid}

    def z_peer(i):
        d = far_first(i, Z)
        return d, z_away(d)

    plane_steps = sorted(
        [(a, b) for a in range(Y) for b in range(C) if a or b],
        key=lambda step: -min(step[0], Y - step[0]),
    )

    def plane_peer(step):
        other = lax.rem(y + step[0], Y) * C + lax.rem(core + step[1], C)
        return other, {"req": z * PL + other}

    def y_peer(i):
        other = lax.rem(y + far_first(i, Y), Y)
        return other, {"req": z * PL + other * C + core}

    def tp_peer(i):
        other = lax.rem(t + far_first(i, T), T)
        return other, {"tp": other}

    core_peer = {"req": z * PL + y * C + (1 - core)}

    def send(src, dst, ssem, rsem, device):
        copy = pltpu.make_async_remote_copy(
            src_ref=src,
            dst_ref=dst,
            send_sem=ssem,
            recv_sem=rsem,
            device_id=device,
            device_id_type=pl.DeviceIdType.MESH,
        )
        copy.start()

    def drain(ref, sem):
        pltpu.make_async_copy(ref, ref, sem).wait()

    def each(count, body):
        def step(d, carry):
            body(d)
            return carry

        lax.fori_loop(1, count, step, 0)

    pairs = [
        (q_hbm, q_ref),
        (k_hbm, k_ref),
        (q_hbm, g0.at[MID, :, pl.ds(0, W)]),
        (v_hbm, g1.at[MID]),
        (res_hbm, g2.at[MID]),
        (owner_hbm, meta_ref.at[0]),
        (order_hbm, meta_ref.at[1]),
        (len_hbm, meta_ref.at[2]),
        (table_hbm, table_ref),
        (kv_hbm, kv),
        (ow_hbm, ow),
        (up_hbm, wts.at[pid, pl.ds(0, FL)]),
        (dw_hbm, wts.at[pid, pl.ds(FL, FL)]),
        (ob_hbm, ob_ref),
        (ng_hbm, ng_ref),
        (nb_hbm, nb_ref),
        (ub_hbm, ub_ref),
        (db_hbm, db_ref),
    ]
    loads = [pltpu.make_async_copy(a, b, local_sem.at[i]) for i, (a, b) in enumerate(pairs)]

    def vector(ref):
        return ref[...].astype(F32).reshape(1, ref.shape[0])

    barrier = pltpu.get_barrier_semaphore()

    def greet(peer):
        def body(d):
            pl.semaphore_signal(
                barrier, inc=1, device_id=peer(d)[1], device_id_type=pl.DeviceIdType.MESH
            )

        return body

    near = [d for r in range(REACH, 0, -1) for d in (r, -r)]
    for d in near:
        greet(lambda d: (d, z_away(d)))(d)
    for step in plane_steps:
        greet(plane_peer)(step)
    each(T, greet(tp_peer))

    for load in loads:
        load.start()

    scale = 1.0 / math.sqrt(HD)
    loads[0].wait()
    loads[1].wait()
    product = q_ref[...].astype(F32) * k_ref[...].astype(F32)
    lane = lax.broadcasted_iota(jnp.int32, (K, HD), 1)
    packed = jnp.zeros((K, HD), F32)
    for h in range(H):
        s = jnp.sum(product[:, h * HD : (h + 1) * HD], axis=1, keepdims=True) * scale
        high = s.astype(BF16).astype(F32)
        mid = (s - high).astype(BF16).astype(F32)
        low = (s - high - mid).astype(BF16).astype(F32)
        packed = jnp.where(lane == h, high, packed)
        packed = jnp.where(lane == H + h, mid, packed)
        packed = jnp.where(lane == 2 * H + h, low, packed)
    g0[MID, :, W : W + HD] = packed.astype(BF16)

    for load in loads[2:5]:
        load.wait()
    pl.semaphore_wait(barrier, len(near) + (PL - 1) + (T - 1))

    sources = (g0, g1, g2)
    for n, source in enumerate(sources):
        for d in near:
            sem = below_r.at[n] if d > 0 else above_r.at[n]
            send(source.at[MID], source.at[MID - d], near_s.at[n], sem, z_away(d))

    def pass_on(n):
        source = sources[n]
        below = source.at[pl.ds(MID - REACH, REACH)]
        drain(below, below_r.at[n])
        send(below, source.at[pl.ds(MID - 2 * REACH, REACH)], far_s.at[n], far_r.at[n], z_away(REACH))
        drain(source.at[pl.ds(MID + 1, REACH)], above_r.at[n])
        if REACH > 1:
            send(
                source.at[pl.ds(MID + 1, REACH - 1)],
                source.at[pl.ds(MID + 1 + REACH, REACH - 1)],
                far_s.at[n],
                far_r.at[n],
                z_away(-REACH),
            )

    for load in [loads[11], loads[12], loads[16]]:
        load.wait()
    spread = hot(iota((FL, W), 1) == pid * FL + iota((FL, W), 0))
    bias8 = jnp.where(iota((8, FL), 0) == 0, vector(ub_ref), 0.0)
    wts[pid, 2 * FL : 2 * FL + 8, :] = jnp.dot(
        bias8.astype(BF16), spread, preferred_element_type=F32
    ).astype(BF16)
    for i in range(1, Y):
        send(wts.at[pid], wts.at[pid], wy_s.at[i], wy_r.at[y], y_peer(i)[1])
    send(wts.at[pid], wts.at[pid], wc_s.at[0], wc_r.at[y], core_peer)

    for load in loads[5:9]:
        load.wait()
    owner_i = meta_ref[0]
    owner_row = owner_i.astype(F32)
    order_i = meta_ref[1]
    len_row = meta_ref[2].astype(F32)

    owners = Z * PL
    lanes = min(R, HD)
    earlier = hot(iota((lanes, lanes), 0) < iota((lanes, lanes), 1))
    ones = jnp.ones((lanes, lanes), BF16)
    before = None
    ranks = []
    for b in range(R // lanes):
        mask = iota((owners, lanes), 0) == owner_i[:, b * lanes : (b + 1) * lanes]
        mask_f = jnp.where(mask, 1.0, 0.0)
        count = jnp.dot(mask_f.astype(BF16), earlier, preferred_element_type=F32)
        if before is not None:
            count = count + jnp.dot(before.astype(BF16), ones, preferred_element_type=F32)
        ranks.append(jnp.sum(mask_f * count, axis=0, keepdims=True))
        before = mask_f if before is None else before + mask_f
    rank_row = jnp.concatenate(ranks, axis=1)

    KL = max(ZK, HD)
    kap = iota((1, KL), 1)
    kap_request = (
        within(over(kap, K) + z + MID, Z) * (PL * K) + pid * K + within(kap, K)
    )
    kap_request = jnp.where(kap < ZK, kap_request, -1)
    pick = hot(iota((R, KL), 0) == kap_request)
    sub8 = iota((8, R), 0)

    def stacked(*rows):
        total = jnp.zeros((8, R), F32)
        for i, row in enumerate(rows):
            total = jnp.where(sub8 == i, row.astype(F32), total)
        return total.astype(BF16)

    picked = jnp.dot(
        stacked(owner_row, rank_row, over(order_i, 16), within(order_i, 16)),
        pick,
        preferred_element_type=F32,
    )
    target = picked[0:1, 0:ZK] * K + picked[1:2, 0:ZK] - (z * (PL * K)).astype(F32)
    sort = hot(iota((PL * K, ZK), 0).astype(F32) == target)
    out_request = (picked[2:3, :] * 16.0 + picked[3:4, :]).astype(jnp.int32)

    for n in range(3):
        pass_on(n)

    def to_plane(n, flat, sendbuf, recvbuf):
        source = sources[n]
        drain(source.at[pl.ds(0, 2 * REACH - 1)], far_r.at[n])
        for s in range(Z):
            flat[s * K : (s + 1) * K, :] = source[s].astype(F32)
        rows = jnp.dot(sort, flat[...].astype(BF16), preferred_element_type=F32)
        for d in range(PL):
            sendbuf[d] = rows[d * K : (d + 1) * K, :].astype(BF16)
        recvbuf[pid] = sendbuf[pid]
        for step in plane_steps:
            other, device = plane_peer(step)
            send(sendbuf.at[other], recvbuf.at[pid], plane_s.at[n], plane_r.at[n], device)
        drain(source.at[pl.ds(0, 2 * REACH)], near_s.at[n])
        drain(source.at[pl.ds(0, 2 * REACH - 1)], far_s.at[n])

    def from_plane(n, recvbuf):
        drain(recvbuf.at[pl.ds(0, PL - 1)], plane_r.at[n])
        total = recvbuf[0].astype(F32)
        for s in range(1, PL):
            total = total + recvbuf[s].astype(F32)
        return total

    to_plane(0, a0, p0, r0)
    for i in range(1, Y):
        other, _ = y_peer(i)
        arrived = wts.at[other * C + core]
        drain(arrived, wy_r.at[other])
        send(arrived, arrived, wc_s.at[i], wc_r.at[other], core_peer)

    mine = (owner_row == me.astype(F32)) & (
        rank_row == sub8.astype(F32)
    )
    mine_f = jnp.where(mine, 1.0, 0.0)
    own_len = jnp.sum(mine_f * len_row, axis=1, keepdims=True)[0:K]
    own_table = lax.dot_general(
        mine_f.astype(BF16),
        table_ref[...].astype(F32).astype(BF16),
        (((1,), (1,)), ((), ())),
        preferred_element_type=F32,
    )[0:K]
    tokens = kv.shape[1]
    page_len = 32
    token = lax.broadcasted_iota(jnp.int32, (1, tokens), 1)
    page = over(token, page_len).astype(F32)
    offset = within(token, page_len).astype(F32)
    len_hk = jnp.concatenate([own_len] * H, axis=0)
    table_hk = jnp.concatenate([own_table] * H, axis=0)
    valid = jnp.zeros((H * K, tokens), F32)
    for j in range(table_ref.shape[0]):
        hit = (table_hk[:, j : j + 1] == page) & (offset + float(j * page_len) < len_hk)
        valid = jnp.where(hit, 1.0, valid)
    valid = valid > 0.5

    to_plane(1, a1, p1, r1)
    to_plane(2, a2, p2, r2)

    own0 = from_plane(0, r0)
    q_own = own0[:, 0:W]
    head_of_row = over(iota((H * K, W), 0), K)
    head_of_lane = over(iota((H * K, W), 1), HD)
    q_block = jnp.where(
        head_of_row == head_of_lane, jnp.concatenate([q_own] * H, axis=0), 0.0
    ).astype(BF16)
    self_col = jnp.concatenate(
        [
            own0[:, W + h : W + h + 1]
            + own0[:, W + H + h : W + H + h + 1]
            + own0[:, W + 2 * H + h : W + 2 * H + h + 1]
            for h in range(H)
        ],
        axis=0,
    )
    loads[9].wait()
    scores = (
        lax.dot_general(q_block, kv[0], (((1,), (1,)), ((), ())), preferred_element_type=F32)
        * scale
    )
    scores = jnp.where(valid, scores, NEG)
    top = jnp.maximum(jnp.max(scores, axis=1, keepdims=True), self_col)
    weights = jnp.where(valid, jnp.exp(scores - top), 0.0)
    self_weight = jnp.exp(self_col - top)
    total = jnp.sum(weights, axis=1, keepdims=True) + self_weight
    wide = jnp.dot(weights.astype(BF16), kv[1], preferred_element_type=F32)
    wide = jnp.where(head_of_row == head_of_lane, wide, 0.0)
    numer = wide[:, 0:HD]
    for h in range(1, H):
        numer = numer + wide[:, h * HD : (h + 1) * HD]

    own1 = from_plane(1, r1)
    v_fold = jnp.concatenate([own1[:, h * HD : (h + 1) * HD] for h in range(H)], axis=0)
    numer = numer + self_weight.astype(BF16).astype(F32) * v_fold
    attn_fold = numer / total
    attn = jnp.concatenate([attn_fold[h * K : (h + 1) * K, :] for h in range(H)], axis=1).astype(
        BF16
    )

    loads[10].wait()
    for load in [loads[13], loads[14], loads[15], loads[17]]:
        load.wait()
    own2 = from_plane(2, r2)
    part[t] = jnp.dot(attn, ow[...], preferred_element_type=F32)
    here = pl.ds(pl.multiple_of(t * W, W), W)
    part[t, :, here] = part[t, :, here] + (own2 + vector(ob_ref))
    each(T, lambda d: send(part.at[t], part.at[t], pt_s, pt_r, tp_peer(d)[1]))
    drain(part.at[pl.ds(0, T - 1)], pt_r)
    summed = part[0]
    for s in range(1, T):
        summed = summed + part[s]
    rows_f = summed.astype(BF16).astype(F32)
    mean = jnp.sum(rows_f, axis=1, keepdims=True) * (1.0 / D)
    centred = rows_f - mean
    var = jnp.sum(centred * centred, axis=1, keepdims=True) * (1.0 / D)
    inverse = lax.rsqrt(var + EPS)
    stream[...] = rows_f
    mine_f32 = stream[:, here]
    nbuf[MID] = ((mine_f32 - mean) * inverse * vector(ng_ref) + vector(nb_ref)).astype(BF16)

    def spread_rows(i):
        d, device = z_peer(i)
        send(nbuf.at[MID], nbuf.at[lax.rem(MID - d + Z, Z)], ng_s, ng_r, device)

    each(Z, spread_rows)

    found = jnp.dot(
        stacked(owner_row, rank_row), hot(iota((R, KL), 0) == out_request), preferred_element_type=F32
    )
    home = found[0:1, :].astype(jnp.int32)
    block = (within(home, C) * Y + within(over(home, C), Y)) * BLK + found[1:2, :].astype(jnp.int32)
    row_at = block + within(over(home, PL) - z + MID + Z, Z) * K
    stream_at = jnp.where(over(home, PL) == z, block + ZK, -1)
    at8 = jnp.where(
        iota((8, KL), 0) == 0,
        row_at.astype(F32),
        stream_at.astype(F32),
    )
    at_col = jnp.transpose(at8)[0:ZK, :]
    lane_a = iota((ZK, PL * BLK), 1).astype(F32)
    choose = jnp.concatenate(
        [hot(lane_a == at_col[:, 0:1]), hot(lane_a == at_col[:, 1:2])], axis=0
    )
    abuf[core, y, ZK:BLK, :] = jnp.concatenate(
        [mine_f32, jnp.zeros((BLK - ZK - K, W), F32)], axis=0
    ).astype(BF16)
    for n, sendbuf in enumerate((p0, p1, p2)):
        drain(sendbuf.at[pl.ds(0, PL - 1)], plane_s.at[n])
    drain(part.at[pl.ds(0, T - 1)], pt_s)

    drain(nbuf.at[pl.ds(0, Z - 1)], ng_r)
    for s in range(Z):
        x32[s * K : (s + 1) * K, :] = nbuf[s].astype(F32)
    for i in range(1, Y + 1):
        if i < Y:
            other, _ = y_peer(i)
            arrived = other * C + (1 - core)
        else:
            arrived = y * C + (1 - core)
            other = y
        drain(wts.at[arrived], wc_r.at[other])

    up = jnp.concatenate([wts[p, 0:FL, :] for p in range(PL)], axis=0)
    hidden = lax.dot_general(
        x32[...].astype(BF16), up, (((1,), (1,)), ((), ())), preferred_element_type=F32
    )
    hbuf[t] = hidden.astype(BF16)
    each(T, lambda d: send(hbuf.at[t], hbuf.at[t], hd_s, hd_r, tp_peer(d)[1]))
    up_bias = wts[0, 2 * FL : 2 * FL + 8, :].astype(F32)
    for p in range(1, PL):
        up_bias = up_bias + wts[p, 2 * FL : 2 * FL + 8, :].astype(F32)
    down = jnp.concatenate([wts[p, FL : 2 * FL, :] for p in range(PL)], axis=0)
    drain(nbuf.at[pl.ds(0, Z - 1)], ng_s)
    for i in range(1, Y):
        drain(wts.at[pid], wy_s.at[i])
    for i in range(Y):
        drain(wts.at[pid], wc_s.at[i])
    drain(hbuf.at[pl.ds(0, T - 1)], hd_r)
    before = hbuf[0].astype(F32)
    for s in range(1, T):
        before = before + hbuf[s].astype(F32)
    before = before + up_bias[0:1, 0 : PL * FL]
    active = 0.5 * before * (1.0 + lax.erf(before * math.sqrt(0.5)))
    abuf[core, y, 0:ZK, 0 : PL * FL] = active.astype(BF16)
    if PL * FL < W:
        abuf[core, y, 0:ZK, PL * FL : W] = jnp.zeros((ZK, W - PL * FL), BF16)

    for i in range(1, Y):
        send(abuf.at[core, y], abuf.at[core, y], ay_s.at[i], ay_r.at[y], y_peer(i)[1])
    send(abuf.at[core, y], abuf.at[core, y], ac_s.at[0], ac_r.at[y], core_peer)
    for i in range(Y - 1, 0, -1):
        other, _ = y_peer(i)
        drain(abuf.at[core, other], ay_r.at[other])
        send(abuf.at[core, other], abuf.at[core, other], ac_s.at[i], ac_r.at[other], core_peer)
    for s in range(Y):
        drain(abuf.at[1 - core, s], ac_r.at[s])

    gathered = jnp.concatenate([abuf[p // Y, p % Y] for p in range(PL)], axis=0)
    chosen = jnp.dot(choose, gathered, preferred_element_type=F32)
    rows = chosen[ZK : 2 * ZK, 0:W] + jnp.dot(
        chosen[0:ZK, 0 : PL * FL].astype(BF16), down, preferred_element_type=F32
    )

    for s in range(Z):
        zsend[s] = rows[s * K : (s + 1) * K, :].astype(BF16)
    zrecv[MID] = zsend[MID]

    def scatter(i):
        d, device = z_peer(i)
        send(
            zsend.at[lax.rem(MID + d, Z)], zrecv.at[lax.rem(MID - d + Z, Z)], fz_s, fz_r, device
        )

    each(Z, scatter)
    drain(hbuf.at[pl.ds(0, T - 1)], hd_s)
    for i in range(1, Y):
        drain(abuf.at[core, y], ay_s.at[i])
    for i in range(Y):
        drain(abuf.at[core, y], ac_s.at[i])
    drain(zrecv.at[pl.ds(0, Z - 1)], fz_r)
    final = zrecv[0].astype(F32)
    for s in range(1, Z):
        final = final + zrecv[s].astype(F32)
    out_ref[...] = (final + vector(db_ref)).astype(BF16)
    drain(zsend.at[pl.ds(0, Z - 1)], fz_s)


def chip_grid(devices):
    cores = 2
    along_y = 4 if devices >= 32 else 2
    return devices // (along_y * cores), along_y, cores


def per_device(
    query,
    key_new,
    value_new,
    resid,
    lengths,
    owner,
    page_table,
    kv_pool,
    out_weight,
    out_bias,
    norm_gain,
    norm_bias,
    up_weight_t,
    up_bias,
    down_weight,
    down_bias,
    order,
):
    K, W = query.shape
    devices = lax.axis_size("req")
    T = lax.axis_size("tp")
    Z, Y, C = chip_grid(devices)
    PL = Y * C
    R = devices * K
    D = W * T
    FL = up_weight_t.shape[0]
    pages, page_len = kv_pool.shape[1], kv_pool.shape[2]
    tokens = pages * page_len
    vmem = pl.BlockSpec(memory_space=pltpu.VMEM)
    hbm = pl.BlockSpec(memory_space=pltpu.HBM)
    dma = pltpu.SemaphoreType.DMA
    return pl.pallas_call(
        functools.partial(layer_kernel, (Z, Y, C, T, W, K)),
        out_shape=jax.ShapeDtypeStruct((K, W), BF16),
        in_specs=[hbm] * 17,
        out_specs=vmem,
        scratch_shapes=[
            pltpu.VMEM((K, W), BF16),
            pltpu.VMEM((K, W), BF16),
            pltpu.VMEM((3, 1, R), jnp.int32),
            pltpu.VMEM((page_table.shape[1], R), jnp.int32),
            pltpu.VMEM((W,), BF16),
            pltpu.VMEM((W,), BF16),
            pltpu.VMEM((W,), BF16),
            pltpu.VMEM((FL,), BF16),
            pltpu.VMEM((W,), BF16),
            pltpu.VMEM((2, tokens, W), BF16),
            pltpu.VMEM((W, D), BF16),
            pltpu.VMEM((PL, 2 * FL + 8, W), BF16),
            pltpu.VMEM((Z, K, W + HD), BF16),
            pltpu.VMEM((Z, K, W), BF16),
            pltpu.VMEM((Z, K, W), BF16),
            pltpu.VMEM((PL, K, W + HD), BF16),
            pltpu.VMEM((PL, K, W), BF16),
            pltpu.VMEM((PL, K, W), BF16),
            pltpu.VMEM((PL, K, W + HD), BF16),
            pltpu.VMEM((PL, K, W), BF16),
            pltpu.VMEM((PL, K, W), BF16),
            pltpu.VMEM((Z * K, W + HD), F32),
            pltpu.VMEM((Z * K, W), F32),
            pltpu.VMEM((Z * K, W), F32),
            pltpu.VMEM((T, K, D), F32),
            pltpu.VMEM((K, D), F32),
            pltpu.VMEM((Z, K, W), BF16),
            pltpu.VMEM((Z * K, W), F32),
            pltpu.VMEM((T, Z * K, PL * FL), BF16),
            pltpu.VMEM((C, Y, Z * K + 8, W), BF16),
            pltpu.VMEM((Z, K, W), BF16),
            pltpu.VMEM((Z, K, W), BF16),
            dma((18,)),
        ]
        + [dma((3,))] * 7
        + [dma(())] * 6
        + [dma((Y,))] * 8
        + [dma(())] * 2,
        compiler_params=pltpu.CompilerParams(
            collective_id=0, has_side_effects=True, vmem_limit_bytes=60 * 1024 * 1024
        ),
    )(
        query,
        key_new,
        value_new,
        resid,
        owner.reshape(1, R),
        order.reshape(1, R),
        lengths.reshape(1, R),
        page_table.T,
        kv_pool.reshape(2, tokens, W),
        out_weight,
        up_weight_t,
        down_weight,
        out_bias,
        norm_gain,
        norm_bias,
        up_bias,
        down_bias,
    )


def solution(mesh):
    in_specs = (
        P("req", "tp"),
        P("req", "tp"),
        P("req", "tp"),
        P("req", "tp"),
        P(),
        P(),
        P(),
        P(None, "req", None, "tp"),
        P("tp", None),
        P("tp"),
        P("tp"),
        P("tp"),
        P("req", "tp"),
        P("req"),
        P("req", "tp"),
        P("tp"),
        P(),
    )
    return jax.shard_map(
        per_device, mesh=mesh, in_specs=in_specs, out_specs=P("req", "tp"), check_vma=False
    )
```

```python
import functools
import math

import jax
import jax.numpy as jnp
from jax import lax
from jax.experimental import pallas as pl
from jax.experimental.pallas import tpu as pltpu
from jax.sharding import PartitionSpec as P

HD = 128
EPS = 1e-05
F32 = jnp.float32
BF16 = jnp.bfloat16
NEG = -1e30


def over(x, n):
    return lax.shift_right_logical(x, n.bit_length() - 1)


def within(x, n):
    return x & (n - 1)


def iota(shape, dim):
    return lax.broadcasted_iota(jnp.int32, shape, dim)


def hot(mask):
    return jnp.where(mask, 1.0, 0.0).astype(BF16)


def layer_kernel(
    dims,
    q_hbm,
    k_hbm,
    v_hbm,
    res_hbm,
    owner_hbm,
    order_hbm,
    len_hbm,
    table_hbm,
    kv_hbm,
    ow_hbm,
    up_hbm,
    dw_hbm,
    ob_hbm,
    ng_hbm,
    nb_hbm,
    ub_hbm,
    db_hbm,
    out_ref,
    q_ref,
    k_ref,
    v_ref,
    res_ref,
    meta_ref,
    table_ref,
    ob_ref,
    ng_ref,
    nb_ref,
    ub_ref,
    db_ref,
    kv,
    ow,
    wts,
    g0,
    g1,
    p0,
    p1,
    r0,
    r1,
    part,
    stream,
    nbuf,
    x32,
    hbuf,
    abuf,
    zsend,
    zrecv,
    local_sem,
    near_s,
    low_r,
    high_r,
    low_edge_r,
    high_edge_r,
    far_s,
    far_r,
    plane_s,
    plane_r,
    pt_s,
    pt_r,
    ng_s,
    ng_r,
    hd_s,
    hd_r,
    wy_s,
    wy_r,
    wc_s,
    wc_r,
    ay_s,
    ay_r,
    ac_s,
    ac_r,
    fz_s,
    fz_r,
):
    Z, Y, C, T, W, K = dims
    PL = Y * C
    R = Z * PL * K
    H = W // HD
    D = W * T
    ZK = Z * K
    FL = up_hbm.shape[0]
    HALF = ZK // 2
    BLK = ZK + 8
    MID = Z // 2
    REACH = Z // 4
    me = lax.axis_index("req")
    t = lax.axis_index("tp")
    core = lax.rem(me, C)
    y = lax.rem(me // C, Y)
    z = me // PL
    pid = lax.rem(me, PL)

    def far_first(i, n):
        return n // 2 + (i // 2) * (1 - 2 * (i % 2))

    def z_away(d):
        return {"req": lax.rem(z + d + Z, Z) * PL + pid}

    def z_peer(i):
        d = far_first(i, Z)
        return d, z_away(d)

    plane_steps = sorted(
        [(a, b) for a in range(Y) for b in range(C) if a or b],
        key=lambda step: -min(step[0], Y - step[0]),
    )

    def plane_peer(step):
        other = lax.rem(y + step[0], Y) * C + lax.rem(core + step[1], C)
        return other, {"req": z * PL + other}

    def y_peer(i):
        other = lax.rem(y + far_first(i, Y), Y)
        return other, {"req": z * PL + other * C + core}

    def tp_peer(i):
        other = lax.rem(t + far_first(i, T), T)
        return other, {"tp": other}

    core_peer = {"req": z * PL + y * C + (1 - core)}

    def send(src, dst, ssem, rsem, device):
        copy = pltpu.make_async_remote_copy(
            src_ref=src,
            dst_ref=dst,
            send_sem=ssem,
            recv_sem=rsem,
            device_id=device,
            device_id_type=pl.DeviceIdType.MESH,
        )
        copy.start()

    def drain(ref, sem):
        pltpu.make_async_copy(ref, ref, sem).wait()

    def each(count, body):
        def step(d, carry):
            body(d)
            return carry

        lax.fori_loop(1, count, step, 0)

    pairs = [
        (q_hbm, q_ref),
        (k_hbm, k_ref),
        (v_hbm, v_ref),
        (res_hbm, res_ref),
        (owner_hbm, meta_ref.at[0]),
        (order_hbm, meta_ref.at[1]),
        (len_hbm, meta_ref.at[2]),
        (table_hbm, table_ref),
        (kv_hbm, kv),
        (ow_hbm, ow),
        (up_hbm, wts.at[pid, pl.ds(0, FL)]),
        (dw_hbm, wts.at[pid, pl.ds(FL, FL)]),
        (ob_hbm, ob_ref),
        (ng_hbm, ng_ref),
        (nb_hbm, nb_ref),
        (ub_hbm, ub_ref),
        (db_hbm, db_ref),
    ]
    loads = [pltpu.make_async_copy(a, b, local_sem.at[i]) for i, (a, b) in enumerate(pairs)]

    def vector(ref):
        return ref[...].astype(F32).reshape(1, ref.shape[0])

    barrier = pltpu.get_barrier_semaphore()

    def greet(peer):
        def body(d):
            pl.semaphore_signal(
                barrier, inc=1, device_id=peer(d)[1], device_id_type=pl.DeviceIdType.MESH
            )

        return body

    near = [d for r in range(REACH, 0, -1) for d in (r, -r)]
    for d in near:
        greet(lambda d: (d, z_away(d)))(d)
    for step in plane_steps:
        greet(plane_peer)(step)
    each(T, greet(tp_peer))

    for load in loads:
        load.start()

    scale = 1.0 / math.sqrt(HD)
    for load in loads[0:4]:
        load.wait()
    product = q_ref[...].astype(F32) * k_ref[...].astype(F32)
    lane = lax.broadcasted_iota(jnp.int32, (K, HD), 1)
    packed = jnp.zeros((K, HD), F32)
    for h in range(H):
        s = jnp.sum(product[:, h * HD : (h + 1) * HD], axis=1, keepdims=True) * scale
        high = s.astype(BF16).astype(F32)
        mid = (s - high).astype(BF16).astype(F32)
        low = (s - high - mid).astype(BF16).astype(F32)
        packed = jnp.where(lane == h, high, packed)
        packed = jnp.where(lane == H + h, mid, packed)
        packed = jnp.where(lane == 2 * H + h, low, packed)
    g0[MID] = jnp.concatenate(
        [
            jnp.concatenate([q_ref[...].astype(F32), packed], axis=1),
            jnp.concatenate([v_ref[...].astype(F32), jnp.zeros((K, HD), F32)], axis=1),
        ],
        axis=0,
    ).astype(BF16)
    own_rest = res_ref[...].astype(F32)
    g1[MID] = jnp.concatenate([own_rest[:, 0 : W // 2], own_rest[:, W // 2 : W]], axis=0).astype(
        BF16
    )

    pl.semaphore_wait(barrier, len(near) + (PL - 1) + (T - 1))

    sources = (g0, g1)
    for n, source in enumerate(sources):
        for d in near:
            if abs(d) == REACH:
                sem = low_edge_r.at[n] if d > 0 else high_edge_r.at[n]
            else:
                sem = low_r.at[n] if d > 0 else high_r.at[n]
            send(source.at[MID], source.at[MID - d], near_s.at[n], sem, z_away(d))

    def pass_on(n):
        source = sources[n]
        low, high = source.at[MID - REACH], source.at[MID + REACH]
        drain(low, low_edge_r.at[n])
        for e in range(REACH, 0, -1):
            send(low, source.at[MID - REACH - e], far_s.at[n], far_r.at[n], z_away(e))
        drain(high, high_edge_r.at[n])
        for e in range(REACH - 1, 0, -1):
            send(high, source.at[MID + REACH + e], far_s.at[n], far_r.at[n], z_away(-e))

    for load in [loads[10], loads[11], loads[15]]:
        load.wait()
    spread = hot(iota((FL, W), 1) == pid * FL + iota((FL, W), 0))
    bias8 = jnp.where(iota((8, FL), 0) == 0, vector(ub_ref), 0.0)
    wts[pid, 2 * FL : 2 * FL + 8, :] = jnp.dot(
        bias8.astype(BF16), spread, preferred_element_type=F32
    ).astype(BF16)
    for i in range(1, Y):
        send(wts.at[pid], wts.at[pid], wy_s.at[i], wy_r.at[y], y_peer(i)[1])
    send(wts.at[pid], wts.at[pid], wc_s.at[0], wc_r.at[y], core_peer)

    for load in loads[4:8]:
        load.wait()
    owner_i = meta_ref[0]
    owner_row = owner_i.astype(F32)
    order_i = meta_ref[1]
    len_row = meta_ref[2].astype(F32)

    owners = Z * PL
    lanes = min(R, HD)
    earlier = hot(iota((lanes, lanes), 0) < iota((lanes, lanes), 1))
    ones = jnp.ones((lanes, lanes), BF16)
    before = None
    ranks = []
    for b in range(R // lanes):
        mask = iota((owners, lanes), 0) == owner_i[:, b * lanes : (b + 1) * lanes]
        mask_f = jnp.where(mask, 1.0, 0.0)
        count = jnp.dot(mask_f.astype(BF16), earlier, preferred_element_type=F32)
        if before is not None:
            count = count + jnp.dot(before.astype(BF16), ones, preferred_element_type=F32)
        ranks.append(jnp.sum(mask_f * count, axis=0, keepdims=True))
        before = mask_f if before is None else before + mask_f
    rank_row = jnp.concatenate(ranks, axis=1)

    KL = max(ZK, HD)
    kap = iota((1, KL), 1)
    out_of = within(over(kap, K) + z - REACH + Z, Z) * (PL * K) + pid * K + within(kap, K)
    pick_out = hot(iota((R, KL), 0) == jnp.where(kap < ZK, out_of, -1))
    tall = iota((1, 2 * ZK), 1)
    row_of = within(over(tall, 2 * K) + z + MID, Z) * (PL * K) + pid * K + within(tall, K)
    pick_row = hot(iota((R, 2 * ZK), 0) == row_of)
    sub8 = iota((8, R), 0)

    def stacked(*rows):
        total = jnp.zeros((8, R), F32)
        for i, row in enumerate(rows):
            total = jnp.where(sub8 == i, row.astype(F32), total)
        return total.astype(BF16)

    picked = jnp.dot(stacked(owner_row, rank_row), pick_row, preferred_element_type=F32)
    target = (
        (picked[0:1, :] - (z * PL).astype(F32)) * (2 * K)
        + picked[1:2, :]
        + (within(over(tall, K), 2) * K).astype(F32)
    )
    sort = hot(iota((PL * 2 * K, 2 * ZK), 0).astype(F32) == target)
    ordered = jnp.dot(
        stacked(over(order_i, 16), within(order_i, 16)), pick_out, preferred_element_type=F32
    )
    out_request = (ordered[0:1, :] * 16.0 + ordered[1:2, :]).astype(jnp.int32)

    for n in range(2):
        pass_on(n)

    def to_plane(n, sendbuf, recvbuf):
        source = sources[n]
        if REACH > 1:
            drain(source.at[pl.ds(MID - REACH + 1, REACH - 1)], low_r.at[n])
            drain(source.at[pl.ds(MID + 1, REACH - 1)], high_r.at[n])
        drain(source.at[pl.ds(0, 2 * REACH - 1)], far_r.at[n])
        rows = jnp.dot(
            sort, source[...].reshape(2 * ZK, source.shape[2]), preferred_element_type=F32
        ).astype(BF16)
        for d in range(PL):
            sendbuf[d] = rows[d * 2 * K : (d + 1) * 2 * K, :]
        recvbuf[pid] = sendbuf[pid]
        for step in plane_steps:
            other, device = plane_peer(step)
            send(sendbuf.at[other], recvbuf.at[pid], plane_s.at[n], plane_r.at[n], device)
        drain(source.at[pl.ds(0, 2 * REACH)], near_s.at[n])
        drain(source.at[pl.ds(0, 2 * REACH - 1)], far_s.at[n])

    def from_plane(n, recvbuf):
        drain(recvbuf.at[pl.ds(0, PL - 1)], plane_r.at[n])
        total = recvbuf[0].astype(F32)
        for s in range(1, PL):
            total = total + recvbuf[s].astype(F32)
        return total

    to_plane(0, p0, r0)
    for i in range(1, Y):
        other, _ = y_peer(i)
        arrived = wts.at[other * C + core]
        drain(arrived, wy_r.at[other])
        send(arrived, arrived, wc_s.at[i], wc_r.at[other], core_peer)

    mine = (owner_row == me.astype(F32)) & (
        rank_row == sub8.astype(F32)
    )
    mine_f = jnp.where(mine, 1.0, 0.0)
    own_len = jnp.sum(mine_f * len_row, axis=1, keepdims=True)[0:K]
    own_table = lax.dot_general(
        mine_f.astype(BF16),
        table_ref[...].astype(F32).astype(BF16),
        (((1,), (1,)), ((), ())),
        preferred_element_type=F32,
    )[0:K]
    tokens = kv.shape[1]
    page_len = 32
    token = lax.broadcasted_iota(jnp.int32, (1, tokens), 1)
    page = over(token, page_len).astype(F32)
    offset = within(token, page_len).astype(F32)
    len_hk = jnp.concatenate([own_len] * H, axis=0)
    table_hk = jnp.concatenate([own_table] * H, axis=0)
    valid = jnp.zeros((H * K, tokens), F32)
    for j in range(table_ref.shape[0]):
        hit = (table_hk[:, j : j + 1] == page) & (offset + float(j * page_len) < len_hk)
        valid = jnp.where(hit, 1.0, valid)
    valid = valid > 0.5

    to_plane(1, p1, r1)

    own0 = from_plane(0, r0)
    q_own = own0[0:K, 0:W]
    v_own = own0[K : 2 * K, 0:W]
    head_of_row = over(iota((H * K, W), 0), K)
    head_of_lane = over(iota((H * K, W), 1), HD)
    q_block = jnp.where(
        head_of_row == head_of_lane, jnp.concatenate([q_own] * H, axis=0), 0.0
    ).astype(BF16)
    self_col = jnp.concatenate(
        [
            own0[0:K, W + h : W + h + 1]
            + own0[0:K, W + H + h : W + H + h + 1]
            + own0[0:K, W + 2 * H + h : W + 2 * H + h + 1]
            for h in range(H)
        ],
        axis=0,
    )
    loads[8].wait()
    scores = (
        lax.dot_general(q_block, kv[0], (((1,), (1,)), ((), ())), preferred_element_type=F32)
        * scale
    )
    scores = jnp.where(valid, scores, NEG)
    top = jnp.maximum(jnp.max(scores, axis=1, keepdims=True), self_col)
    weights = jnp.where(valid, jnp.exp(scores - top), 0.0)
    self_weight = jnp.exp(self_col - top)
    total = jnp.sum(weights, axis=1, keepdims=True) + self_weight
    wide = jnp.dot(weights.astype(BF16), kv[1], preferred_element_type=F32)
    wide = jnp.where(head_of_row == head_of_lane, wide, 0.0)
    numer = wide[:, 0:HD]
    for h in range(1, H):
        numer = numer + wide[:, h * HD : (h + 1) * HD]

    v_fold = jnp.concatenate([v_own[:, h * HD : (h + 1) * HD] for h in range(H)], axis=0)
    numer = numer + self_weight.astype(BF16).astype(F32) * v_fold
    attn_fold = numer / total
    attn = jnp.concatenate([attn_fold[h * K : (h + 1) * K, :] for h in range(H)], axis=1).astype(
        BF16
    )

    loads[9].wait()
    for load in [loads[12], loads[13], loads[14], loads[16]]:
        load.wait()
    part[t] = jnp.dot(attn, ow[...], preferred_element_type=F32)
    own1 = from_plane(1, r1)
    res_own = jnp.concatenate([own1[0:K], own1[K : 2 * K]], axis=1)
    here = pl.ds(pl.multiple_of(t * W, W), W)
    part[t, :, here] = part[t, :, here] + (res_own + vector(ob_ref))
    each(T, lambda d: send(part.at[t], part.at[t], pt_s, pt_r, tp_peer(d)[1]))
    drain(part.at[pl.ds(0, T - 1)], pt_r)
    summed = part[0]
    for s in range(1, T):
        summed = summed + part[s]
    rows_f = summed.astype(BF16).astype(F32)
    mean = jnp.sum(rows_f, axis=1, keepdims=True) * (1.0 / D)
    centred = rows_f - mean
    var = jnp.sum(centred * centred, axis=1, keepdims=True) * (1.0 / D)
    inverse = lax.rsqrt(var + EPS)
    stream[...] = rows_f
    mine_f32 = stream[:, here]
    nbuf[REACH] = ((mine_f32 - mean) * inverse * vector(ng_ref) + vector(nb_ref)).astype(BF16)

    for i in range(1, Z):
        d, device = z_peer(i)
        far = 1 if REACH < d < Z - REACH + 1 else 0
        send(nbuf.at[REACH], nbuf.at[(REACH - d) % Z], ng_s, ng_r.at[far], device)

    found = jnp.dot(
        stacked(owner_row, rank_row), hot(iota((R, KL), 0) == out_request), preferred_element_type=F32
    )
    home = found[0:1, :].astype(jnp.int32)
    block = (within(home, C) * Y + within(over(home, C), Y)) * BLK + found[1:2, :].astype(jnp.int32)
    away = within(over(home, PL) - z + REACH + Z, Z) * K
    row_at = block + away + jnp.where(away < HALF, 0, 8)
    stream_at = jnp.where(over(home, PL) == z, block + HALF, -1)
    at8 = jnp.where(
        iota((8, KL), 0) == 0,
        row_at.astype(F32),
        stream_at.astype(F32),
    )
    at_col = jnp.transpose(at8)[0:ZK, :]
    lane_a = iota((ZK, PL * BLK), 1).astype(F32)
    choose = jnp.concatenate(
        [hot(lane_a == at_col[:, 0:1]), hot(lane_a == at_col[:, 1:2])], axis=0
    )
    abuf[core, y, HALF : HALF + 8, :] = jnp.concatenate(
        [mine_f32, jnp.zeros((8 - K, W), F32)], axis=0
    ).astype(BF16)
    for n, sendbuf in enumerate((p0, p1)):
        drain(sendbuf.at[pl.ds(0, PL - 1)], plane_s.at[n])

    for i in range(1, Y + 1):
        if i < Y:
            other, _ = y_peer(i)
            arrived = other * C + (1 - core)
        else:
            arrived = y * C + (1 - core)
            other = y
        drain(wts.at[arrived], wc_r.at[other])

    up = jnp.concatenate([wts[p, 0:FL, :] for p in range(PL)], axis=0)
    halves = (
        (pl.ds(0, HALF), pl.ds(0, HALF + 8), pl.ds(0, HALF)),
        (pl.ds(HALF, HALF), pl.ds(HALF + 8, HALF), pl.ds(HALF + 8, HALF)),
    )
    drain(part.at[pl.ds(0, T - 1)], pt_s)
    for n, (rows_n, _, _) in enumerate(halves):
        drain(nbuf.at[pl.ds(0, 2 * REACH - 1 + n)], ng_r.at[n])
        first = n * (Z // 2)
        for s in range(first, first + Z // 2):
            x32[s * K : (s + 1) * K, :] = nbuf[s].astype(F32)
        hidden = lax.dot_general(
            x32[rows_n, :].astype(BF16), up, (((1,), (1,)), ((), ())), preferred_element_type=F32
        )
        hbuf[t, rows_n, :] = hidden.astype(BF16)
        for i in range(1, T):
            block_t = hbuf.at[t, rows_n]
            send(block_t, block_t, hd_s.at[n], hd_r.at[n], tp_peer(i)[1])
    up_bias = wts[0, 2 * FL : 2 * FL + 8, :].astype(F32)
    for p in range(1, PL):
        up_bias = up_bias + wts[p, 2 * FL : 2 * FL + 8, :].astype(F32)
    down = jnp.concatenate([wts[p, FL : 2 * FL, :] for p in range(PL)], axis=0)
    drain(nbuf.at[pl.ds(0, Z - 1)], ng_s)
    for i in range(1, Y):
        drain(wts.at[pid], wy_s.at[i])
    for i in range(Y):
        drain(wts.at[pid], wc_s.at[i])
    for n, (rows_n, sent_n, at_n) in enumerate(halves):
        drain(hbuf.at[pl.ds(0, T - 1), rows_n], hd_r.at[n])
        before = hbuf[0, rows_n, :].astype(F32)
        for s in range(1, T):
            before = before + hbuf[s, rows_n, :].astype(F32)
        before = before + up_bias[0:1, 0 : PL * FL]
        active = 0.5 * before * (1.0 + lax.erf(before * math.sqrt(0.5)))
        abuf[core, y, at_n, 0 : PL * FL] = active.astype(BF16)
        if PL * FL < W:
            abuf[core, y, at_n, PL * FL : W] = jnp.zeros((HALF, W - PL * FL), BF16)
        own_block = abuf.at[core, y, sent_n]
        for i in range(1, Y):
            send(own_block, own_block, ay_s.at[n, i], ay_r.at[n, y], y_peer(i)[1])
        send(own_block, own_block, ac_s.at[n, 0], ac_r.at[n, y], core_peer)
    for n, (_, sent_n, _) in enumerate(halves):
        for i in range(Y - 1, 0, -1):
            other, _ = y_peer(i)
            block_n = abuf.at[core, other, sent_n]
            drain(block_n, ay_r.at[n, other])
            send(block_n, block_n, ac_s.at[n, i], ac_r.at[n, other], core_peer)
    for n, (_, sent_n, _) in enumerate(halves):
        for s in range(Y):
            drain(abuf.at[1 - core, s, sent_n], ac_r.at[n, s])

    gathered = jnp.concatenate([abuf[p // Y, p % Y] for p in range(PL)], axis=0)
    chosen = jnp.dot(choose, gathered, preferred_element_type=F32)
    rows = chosen[ZK : 2 * ZK, 0:W] + jnp.dot(
        chosen[0:ZK, 0 : PL * FL].astype(BF16), down, preferred_element_type=F32
    )

    for s in range(Z):
        zsend[s] = rows[s * K : (s + 1) * K, :].astype(BF16)
    zrecv[REACH] = zsend[REACH]
    for i in range(1, Z):
        d, device = z_peer(i)
        send(zsend.at[(REACH + d) % Z], zrecv.at[(REACH - d) % Z], fz_s, fz_r, device)
    for n, (rows_n, sent_n, _) in enumerate(halves):
        drain(hbuf.at[pl.ds(0, T - 1), rows_n], hd_s.at[n])
        for i in range(1, Y):
            drain(abuf.at[core, y, sent_n], ay_s.at[n, i])
        for i in range(Y):
            drain(abuf.at[core, y, sent_n], ac_s.at[n, i])
    drain(zrecv.at[pl.ds(0, Z - 1)], fz_r)
    final = zrecv[0].astype(F32)
    for s in range(1, Z):
        final = final + zrecv[s].astype(F32)
    out_ref[...] = (final + vector(db_ref)).astype(BF16)
    drain(zsend.at[pl.ds(0, Z - 1)], fz_s)


def chip_grid(devices):
    cores = 2
    along_y = 4 if devices >= 32 else 2
    return devices // (along_y * cores), along_y, cores


def per_device(
    query,
    key_new,
    value_new,
    resid,
    lengths,
    owner,
    page_table,
    kv_pool,
    out_weight,
    out_bias,
    norm_gain,
    norm_bias,
    up_weight_t,
    up_bias,
    down_weight,
    down_bias,
    order,
):
    K, W = query.shape
    devices = lax.axis_size("req")
    T = lax.axis_size("tp")
    Z, Y, C = chip_grid(devices)
    PL = Y * C
    R = devices * K
    D = W * T
    FL = up_weight_t.shape[0]
    pages, page_len = kv_pool.shape[1], kv_pool.shape[2]
    tokens = pages * page_len
    vmem = pl.BlockSpec(memory_space=pltpu.VMEM)
    hbm = pl.BlockSpec(memory_space=pltpu.HBM)
    dma = pltpu.SemaphoreType.DMA
    return pl.pallas_call(
        functools.partial(layer_kernel, (Z, Y, C, T, W, K)),
        out_shape=jax.ShapeDtypeStruct((K, W), BF16),
        in_specs=[hbm] * 17,
        out_specs=vmem,
        scratch_shapes=[
            pltpu.VMEM((K, W), BF16),
            pltpu.VMEM((K, W), BF16),
            pltpu.VMEM((K, W), BF16),
            pltpu.VMEM((K, W), BF16),
            pltpu.VMEM((3, 1, R), jnp.int32),
            pltpu.VMEM((page_table.shape[1], R), jnp.int32),
            pltpu.VMEM((W,), BF16),
            pltpu.VMEM((W,), BF16),
            pltpu.VMEM((W,), BF16),
            pltpu.VMEM((FL,), BF16),
            pltpu.VMEM((W,), BF16),
            pltpu.VMEM((2, tokens, W), BF16),
            pltpu.VMEM((W, D), BF16),
            pltpu.VMEM((PL, 2 * FL + 8, W), BF16),
            pltpu.VMEM((Z, 2 * K, W + HD), BF16),
            pltpu.VMEM((Z, 2 * K, W // 2), BF16),
            pltpu.VMEM((PL, 2 * K, W + HD), BF16),
            pltpu.VMEM((PL, 2 * K, W // 2), BF16),
            pltpu.VMEM((PL, 2 * K, W + HD), BF16),
            pltpu.VMEM((PL, 2 * K, W // 2), BF16),
            pltpu.VMEM((T, K, D), F32),
            pltpu.VMEM((K, D), F32),
            pltpu.VMEM((Z, K, W), BF16),
            pltpu.VMEM((Z * K, W), F32),
            pltpu.VMEM((T, Z * K, PL * FL), BF16),
            pltpu.VMEM((C, Y, Z * K + 8, W), BF16),
            pltpu.VMEM((Z, K, W), BF16),
            pltpu.VMEM((Z, K, W), BF16),
            dma((17,)),
        ]
        + [dma((2,))] * 9
        + [dma(())] * 3
        + [dma((2,))] * 3
        + [dma((Y,))] * 4
        + [dma((2, Y))] * 4
        + [dma(())] * 2,
        compiler_params=pltpu.CompilerParams(
            collective_id=0, has_side_effects=True, vmem_limit_bytes=60 * 1024 * 1024
        ),
    )(
        query,
        key_new,
        value_new,
        resid,
        owner.reshape(1, R),
        order.reshape(1, R),
        lengths.reshape(1, R),
        page_table.T,
        kv_pool.reshape(2, tokens, W),
        out_weight,
        up_weight_t,
        down_weight,
        out_bias,
        norm_gain,
        norm_bias,
        up_bias,
        down_bias,
    )


def solution(mesh):
    in_specs = (
        P("req", "tp"),
        P("req", "tp"),
        P("req", "tp"),
        P("req", "tp"),
        P(),
        P(),
        P(),
        P(None, "req", None, "tp"),
        P("tp", None),
        P("tp"),
        P("tp"),
        P("tp"),
        P("req", "tp"),
        P("req"),
        P("req", "tp"),
        P("tp"),
        P(),
    )
    return jax.shard_map(
        per_device, mesh=mesh, in_specs=in_specs, out_specs=P("req", "tp"), check_vma=False
    )
```

```python
import functools
import math

import jax
import jax.numpy as jnp
from jax import lax
from jax.experimental import pallas as pl
from jax.experimental.pallas import tpu as pltpu
from jax.sharding import PartitionSpec as P

HD = 128
EPS = 1e-05
F32 = jnp.float32
BF16 = jnp.bfloat16
NEG = -1e30


def over(x, n):
    return lax.shift_right_logical(x, n.bit_length() - 1)


def within(x, n):
    return x & (n - 1)


def iota(shape, dim):
    return lax.broadcasted_iota(jnp.int32, shape, dim)


def hot(mask):
    return jnp.where(mask, 1.0, 0.0).astype(BF16)


def layer_kernel(
    dims,
    q_hbm,
    k_hbm,
    v_hbm,
    res_hbm,
    owner_hbm,
    order_hbm,
    len_hbm,
    table_hbm,
    kv_hbm,
    ow_hbm,
    up_hbm,
    dw_hbm,
    ob_hbm,
    ng_hbm,
    nb_hbm,
    ub_hbm,
    db_hbm,
    out_ref,
    q_ref,
    k_ref,
    v_ref,
    res_ref,
    meta_ref,
    table_ref,
    ob_ref,
    ng_ref,
    nb_ref,
    ub_ref,
    db_ref,
    kv,
    ow,
    wts,
    g0,
    g1,
    p0,
    p1,
    r0,
    r1,
    part,
    stream,
    nbuf,
    x32,
    hbuf,
    abuf,
    zsend,
    zrecv,
    local_sem,
    near_s,
    low_r,
    high_r,
    low_edge_r,
    high_edge_r,
    far_s,
    far_r,
    plane_s,
    plane_r,
    pt_s,
    pt_r,
    ng_s,
    ng_r,
    hd_s,
    hd_r,
    wy_s,
    wy_r,
    wc_s,
    wc_r,
    ay_s,
    ay_r,
    ac_s,
    ac_r,
    fz_s,
    fz_r,
):
    Z, Y, C, T, W, K = dims
    PL = Y * C
    R = Z * PL * K
    H = W // HD
    D = W * T
    ZK = Z * K
    FL = up_hbm.shape[0]
    HALF = ZK // 2
    groups = ((0, Z // 2), (Z // 2, Z // 4), (3 * Z // 4, Z // 4))
    BLK = ZK + 8
    MID = Z // 2
    REACH = Z // 4
    me = lax.axis_index("req")
    t = lax.axis_index("tp")
    core = lax.rem(me, C)
    y = lax.rem(me // C, Y)
    z = me // PL
    pid = lax.rem(me, PL)

    def far_first(i, n):
        return n // 2 + (i // 2) * (1 - 2 * (i % 2))

    def z_away(d):
        return {"req": lax.rem(z + d + Z, Z) * PL + pid}

    def z_peer(i):
        d = far_first(i, Z)
        return d, z_away(d)

    plane_steps = sorted(
        [(a, b) for a in range(Y) for b in range(C) if a or b],
        key=lambda step: -min(step[0], Y - step[0]),
    )

    def plane_peer(step):
        other = lax.rem(y + step[0], Y) * C + lax.rem(core + step[1], C)
        return other, {"req": z * PL + other}

    def y_peer(i):
        other = lax.rem(y + far_first(i, Y), Y)
        return other, {"req": z * PL + other * C + core}

    def tp_peer(i):
        other = lax.rem(t + far_first(i, T), T)
        return other, {"tp": other}

    core_peer = {"req": z * PL + y * C + (1 - core)}

    def send(src, dst, ssem, rsem, device):
        copy = pltpu.make_async_remote_copy(
            src_ref=src,
            dst_ref=dst,
            send_sem=ssem,
            recv_sem=rsem,
            device_id=device,
            device_id_type=pl.DeviceIdType.MESH,
        )
        copy.start()

    def drain(ref, sem):
        pltpu.make_async_copy(ref, ref, sem).wait()

    def each(count, body):
        def step(d, carry):
            body(d)
            return carry

        lax.fori_loop(1, count, step, 0)

    pairs = [
        (q_hbm, q_ref),
        (k_hbm, k_ref),
        (v_hbm, v_ref),
        (res_hbm, res_ref),
        (owner_hbm, meta_ref.at[0]),
        (order_hbm, meta_ref.at[1]),
        (len_hbm, meta_ref.at[2]),
        (table_hbm, table_ref),
        (kv_hbm, kv),
        (ow_hbm, ow),
        (up_hbm, wts.at[pid, pl.ds(0, FL)]),
        (dw_hbm, wts.at[pid, pl.ds(FL, FL)]),
        (ob_hbm, ob_ref),
        (ng_hbm, ng_ref),
        (nb_hbm, nb_ref),
        (ub_hbm, ub_ref),
        (db_hbm, db_ref),
    ]
    loads = [pltpu.make_async_copy(a, b, local_sem.at[i]) for i, (a, b) in enumerate(pairs)]

    def vector(ref):
        return ref[...].astype(F32).reshape(1, ref.shape[0])

    barrier = pltpu.get_barrier_semaphore()

    def greet(peer):
        def body(d):
            pl.semaphore_signal(
                barrier, inc=1, device_id=peer(d)[1], device_id_type=pl.DeviceIdType.MESH
            )

        return body

    near = [d for r in range(REACH, 0, -1) for d in (r, -r)]
    for d in near:
        greet(lambda d: (d, z_away(d)))(d)
    for step in plane_steps:
        greet(plane_peer)(step)
    each(T, greet(tp_peer))

    for load in loads:
        load.start()

    scale = 1.0 / math.sqrt(HD)
    for load in loads[0:4]:
        load.wait()
    product = q_ref[...].astype(F32) * k_ref[...].astype(F32)
    lane = lax.broadcasted_iota(jnp.int32, (K, HD), 1)
    packed = jnp.zeros((K, HD), F32)
    for h in range(H):
        s = jnp.sum(product[:, h * HD : (h + 1) * HD], axis=1, keepdims=True) * scale
        high = s.astype(BF16).astype(F32)
        mid = (s - high).astype(BF16).astype(F32)
        low = (s - high - mid).astype(BF16).astype(F32)
        packed = jnp.where(lane == h, high, packed)
        packed = jnp.where(lane == H + h, mid, packed)
        packed = jnp.where(lane == 2 * H + h, low, packed)
    g0[MID] = jnp.concatenate(
        [
            jnp.concatenate([q_ref[...].astype(F32), packed], axis=1),
            jnp.concatenate([v_ref[...].astype(F32), jnp.zeros((K, HD), F32)], axis=1),
        ],
        axis=0,
    ).astype(BF16)
    own_rest = res_ref[...].astype(F32)
    g1[MID] = jnp.concatenate([own_rest[:, 0 : W // 2], own_rest[:, W // 2 : W]], axis=0).astype(
        BF16
    )

    for load in loads[4:8]:
        load.wait()
    owner_i = meta_ref[0]
    owner_row = owner_i.astype(F32)
    order_i = meta_ref[1]
    len_row = meta_ref[2].astype(F32)

    owners = Z * PL
    lanes = min(R, HD)
    earlier = hot(iota((lanes, lanes), 0) < iota((lanes, lanes), 1))
    ones = jnp.ones((lanes, lanes), BF16)
    before = None
    ranks = []
    for b in range(R // lanes):
        mask = iota((owners, lanes), 0) == owner_i[:, b * lanes : (b + 1) * lanes]
        mask_f = jnp.where(mask, 1.0, 0.0)
        count = jnp.dot(mask_f.astype(BF16), earlier, preferred_element_type=F32)
        if before is not None:
            count = count + jnp.dot(before.astype(BF16), ones, preferred_element_type=F32)
        ranks.append(jnp.sum(mask_f * count, axis=0, keepdims=True))
        before = mask_f if before is None else before + mask_f
    rank_row = jnp.concatenate(ranks, axis=1)

    KL = max(ZK, HD)
    kap = iota((1, KL), 1)
    out_of = within(over(kap, K) + z - REACH + Z, Z) * (PL * K) + pid * K + within(kap, K)
    pick_out = hot(iota((R, KL), 0) == jnp.where(kap < ZK, out_of, -1))
    tall = iota((1, 2 * ZK), 1)
    row_of = within(over(tall, 2 * K) + z + MID, Z) * (PL * K) + pid * K + within(tall, K)
    pick_row = hot(iota((R, 2 * ZK), 0) == row_of)
    sub8 = iota((8, R), 0)

    def stacked(*rows):
        total = jnp.zeros((8, R), F32)
        for i, row in enumerate(rows):
            total = jnp.where(sub8 == i, row.astype(F32), total)
        return total.astype(BF16)

    picked = jnp.dot(stacked(owner_row, rank_row), pick_row, preferred_element_type=F32)
    target = (
        (picked[0:1, :] - (z * PL).astype(F32)) * (2 * K)
        + picked[1:2, :]
        + (within(over(tall, K), 2) * K).astype(F32)
    )
    sort = hot(iota((PL * 2 * K, 2 * ZK), 0).astype(F32) == target)
    ordered = jnp.dot(
        stacked(over(order_i, 16), within(order_i, 16)), pick_out, preferred_element_type=F32
    )
    out_request = (ordered[0:1, :] * 16.0 + ordered[1:2, :]).astype(jnp.int32)


    pl.semaphore_wait(barrier, len(near) + (PL - 1) + (T - 1))

    sources = (g0, g1)
    for n, source in enumerate(sources):
        for d in near:
            if abs(d) == REACH:
                sem = low_edge_r.at[n] if d > 0 else high_edge_r.at[n]
            else:
                sem = low_r.at[n] if d > 0 else high_r.at[n]
            send(source.at[MID], source.at[MID - d], near_s.at[n], sem, z_away(d))

    def pass_on(n):
        source = sources[n]
        low, high = source.at[MID - REACH], source.at[MID + REACH]
        drain(low, low_edge_r.at[n])
        for e in range(REACH, 0, -1):
            send(low, source.at[MID - REACH - e], far_s.at[n], far_r.at[n], z_away(e))
        drain(high, high_edge_r.at[n])
        for e in range(REACH - 1, 0, -1):
            send(high, source.at[MID + REACH + e], far_s.at[n], far_r.at[n], z_away(-e))

    for load in [loads[10], loads[11], loads[15]]:
        load.wait()
    spread = hot(iota((FL, W), 1) == pid * FL + iota((FL, W), 0))
    bias8 = jnp.where(iota((8, FL), 0) == 0, vector(ub_ref), 0.0)
    wts[pid, 2 * FL : 2 * FL + 8, :] = jnp.dot(
        bias8.astype(BF16), spread, preferred_element_type=F32
    ).astype(BF16)
    for i in range(1, Y):
        send(wts.at[pid], wts.at[pid], wy_s.at[i], wy_r.at[y], y_peer(i)[1])
    send(wts.at[pid], wts.at[pid], wc_s.at[0], wc_r.at[y], core_peer)

    for n in range(2):
        pass_on(n)
    def to_plane(n, sendbuf, recvbuf):
        source = sources[n]
        if REACH > 1:
            drain(source.at[pl.ds(MID - REACH + 1, REACH - 1)], low_r.at[n])
            drain(source.at[pl.ds(MID + 1, REACH - 1)], high_r.at[n])
        drain(source.at[pl.ds(0, 2 * REACH - 1)], far_r.at[n])
        rows = jnp.dot(
            sort, source[...].reshape(2 * ZK, source.shape[2]), preferred_element_type=F32
        ).astype(BF16)
        for d in range(PL):
            sendbuf[d] = rows[d * 2 * K : (d + 1) * 2 * K, :]
        recvbuf[pid] = sendbuf[pid]
        for step in plane_steps:
            other, device = plane_peer(step)
            send(sendbuf.at[other], recvbuf.at[pid], plane_s.at[n], plane_r.at[n], device)
        drain(source.at[pl.ds(0, 2 * REACH)], near_s.at[n])
        drain(source.at[pl.ds(0, 2 * REACH - 1)], far_s.at[n])

    def from_plane(n, recvbuf):
        drain(recvbuf.at[pl.ds(0, PL - 1)], plane_r.at[n])
        total = recvbuf[0].astype(F32)
        for s in range(1, PL):
            total = total + recvbuf[s].astype(F32)
        return total

    to_plane(0, p0, r0)
    for i in range(1, Y):
        other, _ = y_peer(i)
        arrived = wts.at[other * C + core]
        drain(arrived, wy_r.at[other])
        send(arrived, arrived, wc_s.at[i], wc_r.at[other], core_peer)

    mine = (owner_row == me.astype(F32)) & (
        rank_row == sub8.astype(F32)
    )
    mine_f = jnp.where(mine, 1.0, 0.0)
    own_len = jnp.sum(mine_f * len_row, axis=1, keepdims=True)[0:K]
    own_table = lax.dot_general(
        mine_f.astype(BF16),
        table_ref[...].astype(F32).astype(BF16),
        (((1,), (1,)), ((), ())),
        preferred_element_type=F32,
    )[0:K]
    tokens = kv.shape[1]
    page_len = 32
    token = lax.broadcasted_iota(jnp.int32, (1, tokens), 1)
    page = over(token, page_len).astype(F32)
    offset = within(token, page_len).astype(F32)
    len_hk = jnp.concatenate([own_len] * H, axis=0)
    table_hk = jnp.concatenate([own_table] * H, axis=0)
    valid = jnp.zeros((H * K, tokens), F32)
    for j in range(table_ref.shape[0]):
        hit = (table_hk[:, j : j + 1] == page) & (offset + float(j * page_len) < len_hk)
        valid = jnp.where(hit, 1.0, valid)
    valid = valid > 0.5

    to_plane(1, p1, r1)

    own0 = from_plane(0, r0)
    q_own = own0[0:K, 0:W]
    v_own = own0[K : 2 * K, 0:W]
    head_of_row = over(iota((H * K, W), 0), K)
    head_of_lane = over(iota((H * K, W), 1), HD)
    q_block = jnp.where(
        head_of_row == head_of_lane, jnp.concatenate([q_own] * H, axis=0), 0.0
    ).astype(BF16)
    self_col = jnp.concatenate(
        [
            own0[0:K, W + h : W + h + 1]
            + own0[0:K, W + H + h : W + H + h + 1]
            + own0[0:K, W + 2 * H + h : W + 2 * H + h + 1]
            for h in range(H)
        ],
        axis=0,
    )
    loads[8].wait()
    scores = (
        lax.dot_general(q_block, kv[0], (((1,), (1,)), ((), ())), preferred_element_type=F32)
        * scale
    )
    scores = jnp.where(valid, scores, NEG)
    top = jnp.maximum(jnp.max(scores, axis=1, keepdims=True), self_col)
    weights = jnp.where(valid, jnp.exp(scores - top), 0.0)
    self_weight = jnp.exp(self_col - top)
    total = jnp.sum(weights, axis=1, keepdims=True) + self_weight
    wide = jnp.dot(weights.astype(BF16), kv[1], preferred_element_type=F32)
    wide = jnp.where(head_of_row == head_of_lane, wide, 0.0)
    numer = wide[:, 0:HD]
    for h in range(1, H):
        numer = numer + wide[:, h * HD : (h + 1) * HD]

    v_fold = jnp.concatenate([v_own[:, h * HD : (h + 1) * HD] for h in range(H)], axis=0)
    numer = numer + self_weight.astype(BF16).astype(F32) * v_fold
    attn_fold = numer / total
    attn = jnp.concatenate([attn_fold[h * K : (h + 1) * K, :] for h in range(H)], axis=1).astype(
        BF16
    )

    loads[9].wait()
    for load in [loads[12], loads[13], loads[14], loads[16]]:
        load.wait()
    own1 = from_plane(1, r1)
    res_own = jnp.concatenate([own1[0:K], own1[K : 2 * K]], axis=1)
    extra = res_own + vector(ob_ref)
    wide_half = D // 2
    for n in range(2):
        cols = pl.ds(n * wide_half, wide_half)
        add = jnp.concatenate(
            [
                jnp.where(t == n * (T // 2) + b, extra, 0.0)
                for b in range(T // 2)
            ],
            axis=1,
        )
        part[t, :, cols] = jnp.dot(attn, ow[:, cols], preferred_element_type=F32) + add
        own_part = part.at[t, :, cols]
        for i in range(1, T):
            send(own_part, own_part, pt_s, pt_r, tp_peer(i)[1])
    here = pl.ds(pl.multiple_of(t * W, W), W)
    drain(part.at[pl.ds(0, T - 1)], pt_r)
    summed = part[0]
    for s in range(1, T):
        summed = summed + part[s]
    rows_f = summed.astype(BF16).astype(F32)
    mean = jnp.sum(rows_f, axis=1, keepdims=True) * (1.0 / D)
    centred = rows_f - mean
    var = jnp.sum(centred * centred, axis=1, keepdims=True) * (1.0 / D)
    inverse = lax.rsqrt(var + EPS)
    stream[...] = rows_f
    mine_f32 = stream[:, here]
    nbuf[REACH] = ((mine_f32 - mean) * inverse * vector(ng_ref) + vector(nb_ref)).astype(BF16)

    for i in range(1, Z):
        d, device = z_peer(i)
        at = (REACH - d) % Z
        group = [n for n, (first, _) in enumerate(groups) if first <= at][-1]
        send(nbuf.at[REACH], nbuf.at[at], ng_s, ng_r.at[group], device)

    found = jnp.dot(
        stacked(owner_row, rank_row), hot(iota((R, KL), 0) == out_request), preferred_element_type=F32
    )
    home = found[0:1, :].astype(jnp.int32)
    block = (within(home, C) * Y + within(over(home, C), Y)) * BLK + found[1:2, :].astype(jnp.int32)
    away = within(over(home, PL) - z + REACH + Z, Z) * K
    row_at = block + away + jnp.where(away < HALF, 0, 8)
    stream_at = jnp.where(over(home, PL) == z, block + HALF, -1)
    at8 = jnp.where(
        iota((8, KL), 0) == 0,
        row_at.astype(F32),
        stream_at.astype(F32),
    )
    at_col = jnp.transpose(at8)[0:ZK, :]
    lane_a = iota((ZK, PL * BLK), 1).astype(F32)
    choose = jnp.concatenate(
        [hot(lane_a == at_col[:, 0:1]), hot(lane_a == at_col[:, 1:2])], axis=0
    )
    abuf[core, y, HALF : HALF + 8, :] = jnp.concatenate(
        [mine_f32, jnp.zeros((8 - K, W), F32)], axis=0
    ).astype(BF16)
    for n, sendbuf in enumerate((p0, p1)):
        drain(sendbuf.at[pl.ds(0, PL - 1)], plane_s.at[n])

    for i in range(1, Y + 1):
        if i < Y:
            other, _ = y_peer(i)
            arrived = other * C + (1 - core)
        else:
            arrived = y * C + (1 - core)
            other = y
        drain(wts.at[arrived], wc_r.at[other])

    up = jnp.concatenate([wts[p, 0:FL, :] for p in range(PL)], axis=0)
    halves = tuple(
        (
            pl.ds(first * K, count * K),
            pl.ds(first * K + (8 if first else 0), count * K + (0 if first else 8)),
            pl.ds(first * K + (8 if first else 0), count * K),
        )
        for first, count in groups
    )
    drain(part.at[pl.ds(0, T - 1)], pt_s)
    for n, (rows_n, _, _) in enumerate(halves):
        first, count = groups[n]
        drain(nbuf.at[pl.ds(0, count if first else count - 1)], ng_r.at[n])
        for s in range(first, first + count):
            x32[s * K : (s + 1) * K, :] = nbuf[s].astype(F32)
        hidden = lax.dot_general(
            x32[rows_n, :].astype(BF16), up, (((1,), (1,)), ((), ())), preferred_element_type=F32
        )
        hbuf[t, rows_n, :] = hidden.astype(BF16)
        for i in range(1, T):
            block_t = hbuf.at[t, rows_n]
            send(block_t, block_t, hd_s.at[n], hd_r.at[n], tp_peer(i)[1])
    up_bias = wts[0, 2 * FL : 2 * FL + 8, :].astype(F32)
    for p in range(1, PL):
        up_bias = up_bias + wts[p, 2 * FL : 2 * FL + 8, :].astype(F32)
    down = jnp.concatenate([wts[p, FL : 2 * FL, :] for p in range(PL)], axis=0)
    drain(nbuf.at[pl.ds(0, Z - 1)], ng_s)
    for i in range(1, Y):
        drain(wts.at[pid], wy_s.at[i])
    for i in range(Y):
        drain(wts.at[pid], wc_s.at[i])
    for n, (rows_n, sent_n, at_n) in enumerate(halves):
        drain(hbuf.at[pl.ds(0, T - 1), rows_n], hd_r.at[n])
        before = hbuf[0, rows_n, :].astype(F32)
        for s in range(1, T):
            before = before + hbuf[s, rows_n, :].astype(F32)
        before = before + up_bias[0:1, 0 : PL * FL]
        active = 0.5 * before * (1.0 + lax.erf(before * math.sqrt(0.5)))
        abuf[core, y, at_n, 0 : PL * FL] = active.astype(BF16)
        if PL * FL < W:
            abuf[core, y, at_n, PL * FL : W] = jnp.zeros(active.shape[:1] + (W - PL * FL,), BF16)
        own_block = abuf.at[core, y, sent_n]
        for i in range(1, Y):
            send(own_block, own_block, ay_s.at[n, i], ay_r.at[n, y], y_peer(i)[1])
        send(own_block, own_block, ac_s.at[n, 0], ac_r.at[n, y], core_peer)
    for n, (_, sent_n, _) in enumerate(halves):
        for i in range(Y - 1, 0, -1):
            other, _ = y_peer(i)
            block_n = abuf.at[core, other, sent_n]
            drain(block_n, ay_r.at[n, other])
            send(block_n, block_n, ac_s.at[n, i], ac_r.at[n, other], core_peer)
    for n, (_, sent_n, _) in enumerate(halves):
        for s in range(Y):
            drain(abuf.at[1 - core, s, sent_n], ac_r.at[n, s])

    gathered = jnp.concatenate([abuf[p // Y, p % Y] for p in range(PL)], axis=0)
    chosen = jnp.dot(choose, gathered, preferred_element_type=F32)
    rows = chosen[ZK : 2 * ZK, 0:W] + jnp.dot(
        chosen[0:ZK, 0 : PL * FL].astype(BF16), down, preferred_element_type=F32
    )

    for s in range(Z):
        zsend[s] = rows[s * K : (s + 1) * K, :].astype(BF16)
    zrecv[REACH] = zsend[REACH]
    for i in range(1, Z):
        d, device = z_peer(i)
        send(zsend.at[(REACH + d) % Z], zrecv.at[(REACH - d) % Z], fz_s, fz_r, device)
    for n, (rows_n, sent_n, _) in enumerate(halves):
        drain(hbuf.at[pl.ds(0, T - 1), rows_n], hd_s.at[n])
        for i in range(1, Y):
            drain(abuf.at[core, y, sent_n], ay_s.at[n, i])
        for i in range(Y):
            drain(abuf.at[core, y, sent_n], ac_s.at[n, i])
    drain(zrecv.at[pl.ds(0, Z - 1)], fz_r)
    final = zrecv[0].astype(F32)
    for s in range(1, Z):
        final = final + zrecv[s].astype(F32)
    out_ref[...] = (final + vector(db_ref)).astype(BF16)
    drain(zsend.at[pl.ds(0, Z - 1)], fz_s)


def chip_grid(devices):
    cores = 2
    along_y = 4 if devices >= 32 else 2
    return devices // (along_y * cores), along_y, cores


def per_device(
    query,
    key_new,
    value_new,
    resid,
    lengths,
    owner,
    page_table,
    kv_pool,
    out_weight,
    out_bias,
    norm_gain,
    norm_bias,
    up_weight_t,
    up_bias,
    down_weight,
    down_bias,
    order,
):
    K, W = query.shape
    devices = lax.axis_size("req")
    T = lax.axis_size("tp")
    Z, Y, C = chip_grid(devices)
    PL = Y * C
    R = devices * K
    D = W * T
    FL = up_weight_t.shape[0]
    pages, page_len = kv_pool.shape[1], kv_pool.shape[2]
    tokens = pages * page_len
    vmem = pl.BlockSpec(memory_space=pltpu.VMEM)
    hbm = pl.BlockSpec(memory_space=pltpu.HBM)
    dma = pltpu.SemaphoreType.DMA
    return pl.pallas_call(
        functools.partial(layer_kernel, (Z, Y, C, T, W, K)),
        out_shape=jax.ShapeDtypeStruct((K, W), BF16),
        in_specs=[hbm] * 17,
        out_specs=vmem,
        scratch_shapes=[
            pltpu.VMEM((K, W), BF16),
            pltpu.VMEM((K, W), BF16),
            pltpu.VMEM((K, W), BF16),
            pltpu.VMEM((K, W), BF16),
            pltpu.VMEM((3, 1, R), jnp.int32),
            pltpu.VMEM((page_table.shape[1], R), jnp.int32),
            pltpu.VMEM((W,), BF16),
            pltpu.VMEM((W,), BF16),
            pltpu.VMEM((W,), BF16),
            pltpu.VMEM((FL,), BF16),
            pltpu.VMEM((W,), BF16),
            pltpu.VMEM((2, tokens, W), BF16),
            pltpu.VMEM((W, D), BF16),
            pltpu.VMEM((PL, 2 * FL + 8, W), BF16),
            pltpu.VMEM((Z, 2 * K, W + HD), BF16),
            pltpu.VMEM((Z, 2 * K, W // 2), BF16),
            pltpu.VMEM((PL, 2 * K, W + HD), BF16),
            pltpu.VMEM((PL, 2 * K, W // 2), BF16),
            pltpu.VMEM((PL, 2 * K, W + HD), BF16),
            pltpu.VMEM((PL, 2 * K, W // 2), BF16),
            pltpu.VMEM((T, K, D), F32),
            pltpu.VMEM((K, D), F32),
            pltpu.VMEM((Z, K, W), BF16),
            pltpu.VMEM((Z * K, W), F32),
            pltpu.VMEM((T, Z * K, PL * FL), BF16),
            pltpu.VMEM((C, Y, Z * K + 8, W), BF16),
            pltpu.VMEM((Z, K, W), BF16),
            pltpu.VMEM((Z, K, W), BF16),
            dma((17,)),
        ]
        + [dma((2,))] * 9
        + [dma(())] * 3
        + [dma((3,))] * 3
        + [dma((Y,))] * 4
        + [dma((3, Y))] * 4
        + [dma(())] * 2,
        compiler_params=pltpu.CompilerParams(
            collective_id=0, has_side_effects=True, vmem_limit_bytes=60 * 1024 * 1024
        ),
    )(
        query,
        key_new,
        value_new,
        resid,
        owner.reshape(1, R),
        order.reshape(1, R),
        lengths.reshape(1, R),
        page_table.T,
        kv_pool.reshape(2, tokens, W),
        out_weight,
        up_weight_t,
        down_weight,
        out_bias,
        norm_gain,
        norm_bias,
        up_bias,
        down_bias,
    )


def solution(mesh):
    in_specs = (
        P("req", "tp"),
        P("req", "tp"),
        P("req", "tp"),
        P("req", "tp"),
        P(),
        P(),
        P(),
        P(None, "req", None, "tp"),
        P("tp", None),
        P("tp"),
        P("tp"),
        P("tp"),
        P("req", "tp"),
        P("req"),
        P("req", "tp"),
        P("tp"),
        P(),
    )
    return jax.shard_map(
        per_device, mesh=mesh, in_specs=in_specs, out_specs=P("req", "tp"), check_vma=False
    )
```

```python
import functools
import math

import jax
import jax.numpy as jnp
from jax import lax
from jax.experimental import pallas as pl
from jax.experimental.pallas import tpu as pltpu
from jax.sharding import PartitionSpec as P

HD = 128
EPS = 1e-05
F32 = jnp.float32
BF16 = jnp.bfloat16
NEG = -1e30


def over(x, n):
    return lax.shift_right_logical(x, n.bit_length() - 1)


def within(x, n):
    return x & (n - 1)


def iota(shape, dim):
    return lax.broadcasted_iota(jnp.int32, shape, dim)


def hot(mask):
    return jnp.where(mask, 1.0, 0.0).astype(BF16)


def layer_kernel(
    dims,
    q_hbm,
    k_hbm,
    v_hbm,
    res_hbm,
    owner_hbm,
    order_hbm,
    len_hbm,
    table_hbm,
    kv_hbm,
    ow_hbm,
    up_hbm,
    dw_hbm,
    ob_hbm,
    ng_hbm,
    nb_hbm,
    ub_hbm,
    db_hbm,
    out_ref,
    q_ref,
    k_ref,
    v_ref,
    res_ref,
    meta_ref,
    table_ref,
    ob_ref,
    ng_ref,
    nb_ref,
    ub_ref,
    db_ref,
    kv,
    ow,
    wts,
    g0,
    g1,
    p0,
    p1,
    r0,
    r1,
    part,
    stream,
    nbuf,
    x32,
    hbuf,
    abuf,
    zsend,
    zrecv,
    local_sem,
    near_s,
    low_r,
    high_r,
    low_edge_r,
    high_edge_r,
    far_s,
    far_r,
    plane_s,
    plane_r,
    pt_s,
    pt_r,
    ng_s,
    ng_r,
    hd_s,
    hd_r,
    wy_s,
    wy_r,
    wc_s,
    wc_r,
    ay_s,
    ay_r,
    ac_s,
    ac_r,
    fz_s,
    fz_r,
):
    Z, Y, C, T, W, K = dims
    PL = Y * C
    R = Z * PL * K
    H = W // HD
    D = W * T
    ZK = Z * K
    FL = up_hbm.shape[0]
    HALF = ZK // 2
    groups = ((0, Z // 2), (Z // 2, Z // 4), (3 * Z // 4, Z // 4))
    BLK = ZK + 8
    MID = Z // 2
    REACH = Z // 4
    me = lax.axis_index("req")
    t = lax.axis_index("tp")
    core = lax.rem(me, C)
    y = lax.rem(me // C, Y)
    z = me // PL
    pid = lax.rem(me, PL)

    def far_first(i, n):
        return n // 2 + (i // 2) * (1 - 2 * (i % 2))

    def z_away(d):
        return {"req": lax.rem(z + d + Z, Z) * PL + pid}

    def z_peer(i):
        d = far_first(i, Z)
        return d, z_away(d)

    plane_steps = sorted(
        [(a, b) for a in range(Y) for b in range(C) if a or b],
        key=lambda step: -min(step[0], Y - step[0]),
    )

    def plane_peer(step):
        other = lax.rem(y + step[0], Y) * C + lax.rem(core + step[1], C)
        return other, {"req": z * PL + other}

    def y_peer(i):
        other = lax.rem(y + far_first(i, Y), Y)
        return other, {"req": z * PL + other * C + core}

    def tp_peer(i):
        other = lax.rem(t + far_first(i, T), T)
        return other, {"tp": other}

    core_peer = {"req": z * PL + y * C + (1 - core)}

    def send(src, dst, ssem, rsem, device):
        copy = pltpu.make_async_remote_copy(
            src_ref=src,
            dst_ref=dst,
            send_sem=ssem,
            recv_sem=rsem,
            device_id=device,
            device_id_type=pl.DeviceIdType.MESH,
        )
        copy.start()

    def drain(ref, sem):
        pltpu.make_async_copy(ref, ref, sem).wait()

    def each(count, body):
        def step(d, carry):
            body(d)
            return carry

        lax.fori_loop(1, count, step, 0)

    pairs = [
        (q_hbm, q_ref),
        (k_hbm, k_ref),
        (v_hbm, v_ref),
        (res_hbm, res_ref),
        (owner_hbm, meta_ref.at[0]),
        (order_hbm, meta_ref.at[1]),
        (len_hbm, meta_ref.at[2]),
        (table_hbm, table_ref),
        (kv_hbm, kv),
        (ow_hbm, ow),
        (up_hbm, wts.at[pid, pl.ds(0, FL)]),
        (dw_hbm, wts.at[pid, pl.ds(FL, FL)]),
        (ob_hbm, ob_ref),
        (ng_hbm, ng_ref),
        (nb_hbm, nb_ref),
        (ub_hbm, ub_ref),
        (db_hbm, db_ref),
    ]
    loads = [pltpu.make_async_copy(a, b, local_sem.at[i]) for i, (a, b) in enumerate(pairs)]

    def vector(ref):
        return ref[...].astype(F32).reshape(1, ref.shape[0])

    barrier = pltpu.get_barrier_semaphore()

    def greet(peer):
        def body(d):
            pl.semaphore_signal(
                barrier, inc=1, device_id=peer(d)[1], device_id_type=pl.DeviceIdType.MESH
            )

        return body

    near = [d for r in range(REACH, 0, -1) for d in (r, -r)]
    for d in near:
        greet(lambda d: (d, z_away(d)))(d)
    for step in plane_steps:
        greet(plane_peer)(step)
    each(T, greet(tp_peer))

    for load in loads:
        load.start()

    scale = 1.0 / math.sqrt(HD)
    for load in loads[0:4]:
        load.wait()
    product = q_ref[...].astype(F32) * k_ref[...].astype(F32)
    lane = lax.broadcasted_iota(jnp.int32, (K, HD), 1)
    packed = jnp.zeros((K, HD), F32)
    for h in range(H):
        s = jnp.sum(product[:, h * HD : (h + 1) * HD], axis=1, keepdims=True) * scale
        high = s.astype(BF16).astype(F32)
        mid = (s - high).astype(BF16).astype(F32)
        low = (s - high - mid).astype(BF16).astype(F32)
        packed = jnp.where(lane == h, high, packed)
        packed = jnp.where(lane == H + h, mid, packed)
        packed = jnp.where(lane == 2 * H + h, low, packed)
    g0[MID] = jnp.concatenate(
        [
            jnp.concatenate([q_ref[...].astype(F32), packed], axis=1),
            jnp.concatenate([v_ref[...].astype(F32), jnp.zeros((K, HD), F32)], axis=1),
        ],
        axis=0,
    ).astype(BF16)
    own_rest = res_ref[...].astype(F32)
    g1[MID] = jnp.concatenate([own_rest[:, 0 : W // 2], own_rest[:, W // 2 : W]], axis=0).astype(
        BF16
    )

    for load in loads[4:8]:
        load.wait()
    owner_i = meta_ref[0]
    owner_row = owner_i.astype(F32)
    order_i = meta_ref[1]
    len_row = meta_ref[2].astype(F32)

    owners = Z * PL
    lanes = min(R, HD)
    earlier = hot(iota((lanes, lanes), 0) < iota((lanes, lanes), 1))
    ones = jnp.ones((lanes, lanes), BF16)
    before = None
    ranks = []
    for b in range(R // lanes):
        mask = iota((owners, lanes), 0) == owner_i[:, b * lanes : (b + 1) * lanes]
        mask_f = jnp.where(mask, 1.0, 0.0)
        count = jnp.dot(mask_f.astype(BF16), earlier, preferred_element_type=F32)
        if before is not None:
            count = count + jnp.dot(before.astype(BF16), ones, preferred_element_type=F32)
        ranks.append(jnp.sum(mask_f * count, axis=0, keepdims=True))
        before = mask_f if before is None else before + mask_f
    rank_row = jnp.concatenate(ranks, axis=1)

    KL = max(ZK, HD)
    kap = iota((1, KL), 1)
    out_of = within(over(kap, K) + z - REACH + Z, Z) * (PL * K) + pid * K + within(kap, K)
    pick_out = hot(iota((R, KL), 0) == jnp.where(kap < ZK, out_of, -1))
    tall = iota((1, 2 * ZK), 1)
    row_of = within(over(tall, 2 * K) + z + MID, Z) * (PL * K) + pid * K + within(tall, K)
    pick_row = hot(iota((R, 2 * ZK), 0) == row_of)
    sub8 = iota((8, R), 0)

    def stacked(*rows):
        total = jnp.zeros((8, R), F32)
        for i, row in enumerate(rows):
            total = jnp.where(sub8 == i, row.astype(F32), total)
        return total.astype(BF16)

    picked = jnp.dot(stacked(owner_row, rank_row), pick_row, preferred_element_type=F32)
    target = (
        (picked[0:1, :] - (z * PL).astype(F32)) * (2 * K)
        + picked[1:2, :]
        + (within(over(tall, K), 2) * K).astype(F32)
    )
    sort = hot(iota((PL * 2 * K, 2 * ZK), 0).astype(F32) == target)
    ordered = jnp.dot(
        stacked(over(order_i, 16), within(order_i, 16)), pick_out, preferred_element_type=F32
    )
    out_request = (ordered[0:1, :] * 16.0 + ordered[1:2, :]).astype(jnp.int32)


    pl.semaphore_wait(barrier, len(near) + (PL - 1) + (T - 1))

    sources = (g0, g1)
    for n, source in enumerate(sources):
        for d in near:
            if abs(d) == REACH:
                sem = low_edge_r.at[n] if d > 0 else high_edge_r.at[n]
            else:
                sem = low_r.at[n] if d > 0 else high_r.at[n]
            send(source.at[MID], source.at[MID - d], near_s.at[n], sem, z_away(d))

    def pass_on(n):
        source = sources[n]
        low, high = source.at[MID - REACH], source.at[MID + REACH]
        drain(low, low_edge_r.at[n])
        for e in range(REACH, 0, -1):
            send(low, source.at[MID - REACH - e], far_s.at[n], far_r.at[n], z_away(e))
        drain(high, high_edge_r.at[n])
        for e in range(REACH - 1, 0, -1):
            send(high, source.at[MID + REACH + e], far_s.at[n], far_r.at[n], z_away(-e))

    for load in [loads[10], loads[11], loads[15]]:
        load.wait()
    spread = hot(iota((FL, W), 1) == pid * FL + iota((FL, W), 0))
    bias8 = jnp.where(iota((8, FL), 0) == 0, vector(ub_ref), 0.0)
    wts[pid, 2 * FL : 2 * FL + 8, :] = jnp.dot(
        bias8.astype(BF16), spread, preferred_element_type=F32
    ).astype(BF16)
    for i in range(1, Y):
        send(wts.at[pid], wts.at[pid], wy_s.at[i], wy_r.at[y], y_peer(i)[1])
    send(wts.at[pid], wts.at[pid], wc_s.at[0], wc_r.at[y], core_peer)

    for n in range(2):
        pass_on(n)
    def to_plane(n, sendbuf, recvbuf):
        source = sources[n]
        if REACH > 1:
            drain(source.at[pl.ds(MID - REACH + 1, REACH - 1)], low_r.at[n])
            drain(source.at[pl.ds(MID + 1, REACH - 1)], high_r.at[n])
        drain(source.at[pl.ds(0, 2 * REACH - 1)], far_r.at[n])
        rows = jnp.dot(
            sort, source[...].reshape(2 * ZK, source.shape[2]), preferred_element_type=F32
        ).astype(BF16)
        for d in range(PL):
            sendbuf[d] = rows[d * 2 * K : (d + 1) * 2 * K, :]
        recvbuf[pid] = sendbuf[pid]
        for step in plane_steps:
            other, device = plane_peer(step)
            send(sendbuf.at[other], recvbuf.at[pid], plane_s.at[n], plane_r.at[n], device)
        drain(source.at[pl.ds(0, 2 * REACH)], near_s.at[n])
        drain(source.at[pl.ds(0, 2 * REACH - 1)], far_s.at[n])

    def from_plane(n, recvbuf):
        drain(recvbuf.at[pl.ds(0, PL - 1)], plane_r.at[n])
        total = recvbuf[0].astype(F32)
        for s in range(1, PL):
            total = total + recvbuf[s].astype(F32)
        return total

    to_plane(0, p0, r0)
    for i in range(1, Y):
        other, _ = y_peer(i)
        arrived = wts.at[other * C + core]
        drain(arrived, wy_r.at[other])
        send(arrived, arrived, wc_s.at[i], wc_r.at[other], core_peer)

    mine = (owner_row == me.astype(F32)) & (
        rank_row == sub8.astype(F32)
    )
    mine_f = jnp.where(mine, 1.0, 0.0)
    own_len = jnp.sum(mine_f * len_row, axis=1, keepdims=True)[0:K]
    own_table = lax.dot_general(
        mine_f.astype(BF16),
        table_ref[...].astype(F32).astype(BF16),
        (((1,), (1,)), ((), ())),
        preferred_element_type=F32,
    )[0:K]
    tokens = kv.shape[1]
    page_len = 32
    token = lax.broadcasted_iota(jnp.int32, (1, tokens), 1)
    page = over(token, page_len).astype(F32)
    offset = within(token, page_len).astype(F32)
    len_hk = jnp.concatenate([own_len] * H, axis=0)
    table_hk = jnp.concatenate([own_table] * H, axis=0)
    valid = jnp.zeros((H * K, tokens), F32)
    for j in range(table_ref.shape[0]):
        hit = (table_hk[:, j : j + 1] == page) & (offset + float(j * page_len) < len_hk)
        valid = jnp.where(hit, 1.0, valid)
    valid = valid > 0.5

    to_plane(1, p1, r1)

    own0 = from_plane(0, r0)
    q_own = own0[0:K, 0:W]
    v_own = own0[K : 2 * K, 0:W]
    head_of_row = over(iota((H * K, W), 0), K)
    head_of_lane = over(iota((H * K, W), 1), HD)
    q_block = jnp.where(
        head_of_row == head_of_lane, jnp.concatenate([q_own] * H, axis=0), 0.0
    ).astype(BF16)
    self_col = jnp.concatenate(
        [
            own0[0:K, W + h : W + h + 1]
            + own0[0:K, W + H + h : W + H + h + 1]
            + own0[0:K, W + 2 * H + h : W + 2 * H + h + 1]
            for h in range(H)
        ],
        axis=0,
    )
    loads[8].wait()
    scores = (
        lax.dot_general(q_block, kv[0], (((1,), (1,)), ((), ())), preferred_element_type=F32)
        * scale
    )
    scores = jnp.where(valid, scores, NEG)
    top = jnp.maximum(jnp.max(scores, axis=1, keepdims=True), self_col)
    weights = jnp.where(valid, jnp.exp(scores - top), 0.0)
    self_weight = jnp.exp(self_col - top)
    total = jnp.sum(weights, axis=1, keepdims=True) + self_weight
    wide = jnp.dot(weights.astype(BF16), kv[1], preferred_element_type=F32)
    wide = jnp.where(head_of_row == head_of_lane, wide, 0.0)
    numer = wide[:, 0:HD]
    for h in range(1, H):
        numer = numer + wide[:, h * HD : (h + 1) * HD]

    v_fold = jnp.concatenate([v_own[:, h * HD : (h + 1) * HD] for h in range(H)], axis=0)
    numer = numer + self_weight.astype(BF16).astype(F32) * v_fold
    attn_fold = numer / total
    attn = jnp.concatenate([attn_fold[h * K : (h + 1) * K, :] for h in range(H)], axis=1).astype(
        BF16
    )

    loads[9].wait()
    for load in [loads[12], loads[13], loads[14], loads[16]]:
        load.wait()
    own1 = from_plane(1, r1)
    res_own = jnp.concatenate([own1[0:K], own1[K : 2 * K]], axis=1)
    extra = res_own + vector(ob_ref)
    wide_half = D // 2
    for n in range(2):
        cols = pl.ds(n * wide_half, wide_half)
        add = jnp.concatenate(
            [
                jnp.where(t == n * (T // 2) + b, extra, 0.0)
                for b in range(T // 2)
            ],
            axis=1,
        )
        part[t, :, cols] = jnp.dot(attn, ow[:, cols], preferred_element_type=F32) + add
        own_part = part.at[t, :, cols]
        for i in range(1, T):
            send(own_part, own_part, pt_s, pt_r, tp_peer(i)[1])
    here = pl.ds(pl.multiple_of(t * W, W), W)
    drain(part.at[pl.ds(0, T - 1)], pt_r)
    summed = part[0]
    for s in range(1, T):
        summed = summed + part[s]
    rows_f = summed.astype(BF16).astype(F32)
    mean = jnp.sum(rows_f, axis=1, keepdims=True) * (1.0 / D)
    centred = rows_f - mean
    var = jnp.sum(centred * centred, axis=1, keepdims=True) * (1.0 / D)
    inverse = lax.rsqrt(var + EPS)
    stream[...] = rows_f
    mine_f32 = stream[:, here]
    nbuf[REACH] = ((mine_f32 - mean) * inverse * vector(ng_ref) + vector(nb_ref)).astype(BF16)

    for i in range(1, Z):
        d, device = z_peer(i)
        at = (REACH - d) % Z
        group = [n for n, (first, _) in enumerate(groups) if first <= at][-1]
        send(nbuf.at[REACH], nbuf.at[at], ng_s, ng_r.at[group], device)

    found = jnp.dot(
        stacked(owner_row, rank_row), hot(iota((R, KL), 0) == out_request), preferred_element_type=F32
    )
    home = found[0:1, :].astype(jnp.int32)
    block = (within(home, C) * Y + within(over(home, C), Y)) * BLK + found[1:2, :].astype(jnp.int32)
    away = within(over(home, PL) - z + REACH + Z, Z) * K
    row_at = block + away + jnp.where(away < HALF, 0, 8)
    stream_at = jnp.where(over(home, PL) == z, block + HALF, -1)
    at8 = jnp.where(
        iota((8, KL), 0) == 0,
        row_at.astype(F32),
        stream_at.astype(F32),
    )
    at_col = jnp.transpose(at8)[0:ZK, :]
    lane_a = iota((ZK, PL * BLK), 1).astype(F32)
    choose = jnp.concatenate(
        [hot(lane_a == at_col[:, 0:1]), hot(lane_a == at_col[:, 1:2])], axis=0
    )
    abuf[core, y, HALF : HALF + 8, :] = jnp.concatenate(
        [mine_f32, jnp.zeros((8 - K, W), F32)], axis=0
    ).astype(BF16)
    for n, sendbuf in enumerate((p0, p1)):
        drain(sendbuf.at[pl.ds(0, PL - 1)], plane_s.at[n])

    for i in range(1, Y + 1):
        if i < Y:
            other, _ = y_peer(i)
            arrived = other * C + (1 - core)
        else:
            arrived = y * C + (1 - core)
            other = y
        drain(wts.at[arrived], wc_r.at[other])

    up = jnp.concatenate([wts[p, 0:FL, :] for p in range(PL)], axis=0)
    halves = tuple(
        (
            pl.ds(first * K, count * K),
            pl.ds(first * K + (8 if first else 0), count * K + (0 if first else 8)),
            pl.ds(first * K + (8 if first else 0), count * K),
        )
        for first, count in groups
    )
    drain(part.at[pl.ds(0, T - 1)], pt_s)
    for n, (rows_n, _, _) in enumerate(halves):
        first, count = groups[n]
        drain(nbuf.at[pl.ds(0, count if first else count - 1)], ng_r.at[n])
        for s in range(first, first + count):
            x32[s * K : (s + 1) * K, :] = nbuf[s].astype(F32)
        hidden = lax.dot_general(
            x32[rows_n, :].astype(BF16), up, (((1,), (1,)), ((), ())), preferred_element_type=F32
        )
        hbuf[t, rows_n, :] = hidden.astype(BF16)
        for i in range(1, T):
            block_t = hbuf.at[t, rows_n]
            send(block_t, block_t, hd_s.at[n], hd_r.at[n], tp_peer(i)[1])
    up_bias = wts[0, 2 * FL : 2 * FL + 8, :].astype(F32)
    for p in range(1, PL):
        up_bias = up_bias + wts[p, 2 * FL : 2 * FL + 8, :].astype(F32)
    down = jnp.concatenate([wts[p, FL : 2 * FL, :] for p in range(PL)], axis=0)
    drain(nbuf.at[pl.ds(0, Z - 1)], ng_s)
    for i in range(1, Y):
        drain(wts.at[pid], wy_s.at[i])
    for i in range(Y):
        drain(wts.at[pid], wc_s.at[i])
    for n, (rows_n, sent_n, at_n) in enumerate(halves):
        drain(hbuf.at[pl.ds(0, T - 1), rows_n], hd_r.at[n])
        before = hbuf[0, rows_n, :].astype(F32)
        for s in range(1, T):
            before = before + hbuf[s, rows_n, :].astype(F32)
        before = before + up_bias[0:1, 0 : PL * FL]
        active = 0.5 * before * (1.0 + lax.erf(before * math.sqrt(0.5)))
        abuf[core, y, at_n, 0 : PL * FL] = active.astype(BF16)
        if PL * FL < W:
            abuf[core, y, at_n, PL * FL : W] = jnp.zeros(active.shape[:1] + (W - PL * FL,), BF16)
        own_block = abuf.at[core, y, sent_n]
        for i in range(1, Y):
            other, device = y_peer(i)
            send(own_block, own_block, ay_s.at[n, i], ay_r.at[n, y], device)
            if n == len(halves) - 1:
                twin = {"req": z * PL + other * C + (1 - core)}
                send(own_block, own_block, ac_s.at[n, i], ac_r.at[n, y], twin)
        send(own_block, own_block, ac_s.at[n, 0], ac_r.at[n, y], core_peer)
    for n, (_, sent_n, _) in enumerate(halves):
        for i in range(Y - 1, 0, -1):
            other, _ = y_peer(i)
            block_n = abuf.at[core, other, sent_n]
            drain(block_n, ay_r.at[n, other])
            if n < len(halves) - 1:
                send(block_n, block_n, ac_s.at[n, i], ac_r.at[n, other], core_peer)
    for n, (_, sent_n, _) in enumerate(halves):
        for s in range(Y):
            drain(abuf.at[1 - core, s, sent_n], ac_r.at[n, s])

    gathered = jnp.concatenate([abuf[p // Y, p % Y] for p in range(PL)], axis=0)
    chosen = jnp.dot(choose, gathered, preferred_element_type=F32)
    rows = chosen[ZK : 2 * ZK, 0:W] + jnp.dot(
        chosen[0:ZK, 0 : PL * FL].astype(BF16), down, preferred_element_type=F32
    )

    for s in range(Z):
        zsend[s] = rows[s * K : (s + 1) * K, :].astype(BF16)
    zrecv[REACH] = zsend[REACH]
    for i in range(1, Z):
        d, device = z_peer(i)
        send(zsend.at[(REACH + d) % Z], zrecv.at[(REACH - d) % Z], fz_s, fz_r, device)
    for n, (rows_n, sent_n, _) in enumerate(halves):
        drain(hbuf.at[pl.ds(0, T - 1), rows_n], hd_s.at[n])
        for i in range(1, Y):
            drain(abuf.at[core, y, sent_n], ay_s.at[n, i])
        for i in range(Y):
            drain(abuf.at[core, y, sent_n], ac_s.at[n, i])
    drain(zrecv.at[pl.ds(0, Z - 1)], fz_r)
    final = zrecv[0].astype(F32)
    for s in range(1, Z):
        final = final + zrecv[s].astype(F32)
    out_ref[...] = (final + vector(db_ref)).astype(BF16)
    drain(zsend.at[pl.ds(0, Z - 1)], fz_s)


def chip_grid(devices):
    cores = 2
    along_y = 4 if devices >= 32 else 2
    return devices // (along_y * cores), along_y, cores


def per_device(
    query,
    key_new,
    value_new,
    resid,
    lengths,
    owner,
    page_table,
    kv_pool,
    out_weight,
    out_bias,
    norm_gain,
    norm_bias,
    up_weight_t,
    up_bias,
    down_weight,
    down_bias,
    order,
):
    K, W = query.shape
    devices = lax.axis_size("req")
    T = lax.axis_size("tp")
    Z, Y, C = chip_grid(devices)
    PL = Y * C
    R = devices * K
    D = W * T
    FL = up_weight_t.shape[0]
    pages, page_len = kv_pool.shape[1], kv_pool.shape[2]
    tokens = pages * page_len
    vmem = pl.BlockSpec(memory_space=pltpu.VMEM)
    hbm = pl.BlockSpec(memory_space=pltpu.HBM)
    dma = pltpu.SemaphoreType.DMA
    return pl.pallas_call(
        functools.partial(layer_kernel, (Z, Y, C, T, W, K)),
        out_shape=jax.ShapeDtypeStruct((K, W), BF16),
        in_specs=[hbm] * 17,
        out_specs=vmem,
        scratch_shapes=[
            pltpu.VMEM((K, W), BF16),
            pltpu.VMEM((K, W), BF16),
            pltpu.VMEM((K, W), BF16),
            pltpu.VMEM((K, W), BF16),
            pltpu.VMEM((3, 1, R), jnp.int32),
            pltpu.VMEM((page_table.shape[1], R), jnp.int32),
            pltpu.VMEM((W,), BF16),
            pltpu.VMEM((W,), BF16),
            pltpu.VMEM((W,), BF16),
            pltpu.VMEM((FL,), BF16),
            pltpu.VMEM((W,), BF16),
            pltpu.VMEM((2, tokens, W), BF16),
            pltpu.VMEM((W, D), BF16),
            pltpu.VMEM((PL, 2 * FL + 8, W), BF16),
            pltpu.VMEM((Z, 2 * K, W + HD), BF16),
            pltpu.VMEM((Z, 2 * K, W // 2), BF16),
            pltpu.VMEM((PL, 2 * K, W + HD), BF16),
            pltpu.VMEM((PL, 2 * K, W // 2), BF16),
            pltpu.VMEM((PL, 2 * K, W + HD), BF16),
            pltpu.VMEM((PL, 2 * K, W // 2), BF16),
            pltpu.VMEM((T, K, D), F32),
            pltpu.VMEM((K, D), F32),
            pltpu.VMEM((Z, K, W), BF16),
            pltpu.VMEM((Z * K, W), F32),
            pltpu.VMEM((T, Z * K, PL * FL), BF16),
            pltpu.VMEM((C, Y, Z * K + 8, W), BF16),
            pltpu.VMEM((Z, K, W), BF16),
            pltpu.VMEM((Z, K, W), BF16),
            dma((17,)),
        ]
        + [dma((2,))] * 9
        + [dma(())] * 3
        + [dma((3,))] * 3
        + [dma((Y,))] * 4
        + [dma((3, Y))] * 4
        + [dma(())] * 2,
        compiler_params=pltpu.CompilerParams(
            collective_id=0, has_side_effects=True, vmem_limit_bytes=60 * 1024 * 1024
        ),
    )(
        query,
        key_new,
        value_new,
        resid,
        owner.reshape(1, R),
        order.reshape(1, R),
        lengths.reshape(1, R),
        page_table.T,
        kv_pool.reshape(2, tokens, W),
        out_weight,
        up_weight_t,
        down_weight,
        out_bias,
        norm_gain,
        norm_bias,
        up_bias,
        down_bias,
    )


def solution(mesh):
    in_specs = (
        P("req", "tp"),
        P("req", "tp"),
        P("req", "tp"),
        P("req", "tp"),
        P(),
        P(),
        P(),
        P(None, "req", None, "tp"),
        P("tp", None),
        P("tp"),
        P("tp"),
        P("tp"),
        P("req", "tp"),
        P("req"),
        P("req", "tp"),
        P("tp"),
        P(),
    )
    return jax.shard_map(
        per_device, mesh=mesh, in_specs=in_specs, out_specs=P("req", "tp"), check_vma=False
    )
```
